512 devices in a mesh: grp: 64 (over x, z), box: 8 (over y, core).
Axes of the slice: x: 4, y: 4, z: 16, core: 2. Of those that a mesh axis runs over, the one named last changes fastest.
Arguments:
- fine_state: float32 [64, 5, 32, 16, 256], P('grp', None, 'box'), may hold values from -1 to 6, as said below
- patch_ghosts: float32 [64, 2, 2, 5, 16, 256], P('grp'), may hold values from -1 to 6, as said below
- coarse_state: float32 [64, 8, 24, 5, 128], P('grp', 'box'), may hold values from -1 to 6, as said below
- coarse_face_term: float32 [64, 8, 24, 5, 128], P('grp', 'box'), may hold values from -1 to 1
- dest_grp: int32 [64, 8, 24], P('grp', 'box'), may hold values from 0 to 63, as said below
- dest_column: int32 [64, 8, 24], P('grp', 'box'), may hold values from 0 to 23, as said below
Outputs:
- fine_new: float32 [64, 5, 32, 16, 256], P('grp', None, 'box')
- coarse_new: float32 [64, 8, 24, 5, 128], P('grp', 'box')
The draws below stay inside these ranges and needn't reach their ends.
Inputs may be any that keep to these rules, and one draw needn't show every extreme that they name: `fine_state`: every cell has density in 1 to 2, velocity components in -0.5 to 0.5 and pressure in 1 to 2. `patch_ghosts`: every cell has density in 1 to 2, velocity components in -0.5 to 0.5 and pressure in 1 to 2. `coarse_state`: every cell has density in 1 to 2, velocity components in -0.5 to 0.5 and pressure in 1 to 2. `dest_grp`: for each box index, each owner's columns receive exactly one record each; one box sends at most 1 and at least 0 records to each owner. `dest_column`: see dest_grp.
All inputs are finite; a program needn't handle non-finite values.
Results may differ from the reference program's by a relative error of at most 0.0001.
Values sent between devices are 32-bit elements; how exact they have to be, the bound alone decides.
A program may use at most 64 MiB of HBM per device.

```python
import jax
import jax.numpy as jnp
from jax import lax

FIELDS = 5
FX = 4
FY = 16
FZ = 256
SUBSTEPS = 2
NXF = 32
CZ = 128
NCOL = 16
REC = 24
N_GRP = 64
N_BOX = 8


def conserved_draw(key, lead_shape, stack_axis):
    subkeys = jax.random.split(key, 5)
    uniforms = [jax.random.uniform(subkeys[member], lead_shape, jnp.float32) for member in range(5)]
    density = 1.0 + uniforms[0]
    velocity = [uniforms[member] - 0.5 for member in (1, 2, 3)]
    pressure = 1.0 + uniforms[4]
    kinetic = 0.5 * density * (velocity[0] ** 2 + velocity[1] ** 2 + velocity[2] ** 2)
    energy = pressure / 0.4 + kinetic
    members = [density, density * velocity[0], density * velocity[1], density * velocity[2], energy]
    return jnp.stack(members, axis=stack_axis)


def draw_fine_state(key, part):
    return conserved_draw(jax.random.fold_in(key, 11), (N_GRP, NXF, FY, FZ), 1)


def draw_patch_ghosts(key, part):
    return conserved_draw(jax.random.fold_in(key, 12), (N_GRP, 2, 2, FY, FZ), 3)


def draw_coarse_state(key, part):
    return conserved_draw(jax.random.fold_in(key, 13), (N_GRP, N_BOX, REC, CZ), 3)


def shuffle_columns(order_key):
    return jax.random.permutation(order_key, REC)


def routing(key):
    base = jax.random.fold_in(key, 7)
    plane_keys = jax.random.split(base, N_BOX)

    def plane(plane_key):
        first, second, third, fourth = jax.random.split(plane_key, 4)
        values = jnp.arange(N_GRP, dtype=jnp.int32)
        scores = jax.random.permutation(first, N_GRP).astype(jnp.int32)
        scores = jnp.where(values == 1, -2, jnp.where(values == N_GRP // 2, -1, scores))
        relabel = jnp.argsort(scores, stable=True).astype(jnp.int32)
        offsets = relabel[jnp.arange(REC) % N_GRP][jax.random.permutation(second, REC)]
        rotate = jax.random.randint(third, (N_GRP,), 0, REC)
        shifted = (jnp.arange(REC)[None, :] + rotate[:, None]) % REC
        owners = (jnp.arange(N_GRP)[:, None] + offsets[shifted]) % N_GRP
        orders = jax.vmap(shuffle_columns)(jax.random.split(fourth, N_GRP))
        columns = orders[owners, shifted]
        return (owners, columns)
    owners, columns = jax.vmap(plane)(plane_keys)
    return (owners.transpose(1, 0, 2).astype(jnp.int32), columns.transpose(1, 0, 2).astype(jnp.int32))


def draw_dest_grp(key, part):
    return routing(key)[0]


def draw_dest_column(key, part):
    return routing(key)[1]


def block_levels(own_key, dims, cuts, least, largest):
    factor_of, own = 1.0, jax.random.fold_in(own_key, 6)
    for axis_at, parts in cuts:
        draws = jnp.exp(jax.random.uniform(jax.random.fold_in(own, axis_at), (parts,), jnp.float32, least / len(cuts), largest / len(cuts)))
        factor_of = factor_of * jnp.repeat(draws, dims[axis_at] // parts).reshape([-1 if axis == axis_at else 1 for axis in range(len(dims))])
    return factor_of


def scatter_about(own_key, shape, scale, bound, cuts=(), kind=jnp.bfloat16):
    array = jax.random.normal(own_key, shape, jnp.float32) * scale
    if len(cuts) > 0:
        array = block_levels(own_key, shape, cuts, -0.22, 0.18) * array
    return jnp.clip(array, min=-bound, max=bound).astype(kind)


def setup_inputs(seed: int = 0) -> dict:
    arg_keys = jax.random.split(jax.random.key(seed), 7)
    return {
        "fine_state": draw_fine_state(jax.random.fold_in(arg_keys[6], 71), 0),
        "patch_ghosts": draw_patch_ghosts(jax.random.fold_in(arg_keys[6], 71), 0),
        "coarse_state": draw_coarse_state(jax.random.fold_in(arg_keys[6], 71), 0),
        "coarse_face_term": scatter_about(arg_keys[3], (N_GRP, N_BOX, REC, FIELDS, CZ), 0.2, 1.0, ((0, 64), (1, 8)), jnp.float32),
        "dest_grp": draw_dest_grp(jax.random.fold_in(arg_keys[6], 71), 0),
        "dest_column": draw_dest_column(jax.random.fold_in(arg_keys[6], 71), 0),
    }


gamma_ratio = 1.4
time_step = 0.06

def cell_values(conserved):
    density = conserved[0]
    velocity = conserved[1:4] / density
    kinetic = 0.5 * lax.optimization_barrier(jnp.sum(conserved[1:4] * velocity, axis=0))
    pressure = (gamma_ratio - 1.0) * (conserved[4] - kinetic)
    sound_speed = jnp.sqrt(gamma_ratio * pressure / density)
    return (velocity, pressure, sound_speed)

def physical_flux(conserved, velocity, pressure, normal):
    moving = velocity[normal]
    pieces = [conserved[1 + normal]]
    for member in range(3):
        if member == normal:
            pieces.append(conserved[1 + member] * moving + pressure)
        else:
            pieces.append(conserved[1 + member] * moving)
    pieces.append((conserved[4] + pressure) * moving)
    return jnp.stack(pieces)

def rusanov(left_state, right_state, left_flux, right_flux, left_speed, right_speed):
    biggest = jnp.maximum(left_speed, right_speed)
    return 0.5 * (left_flux + right_flux) - 0.5 * biggest * (right_state - left_state)

def advance(extended):
    velocity, pressure, sound_speed = cell_values(extended)
    cell_flux = physical_flux(extended, velocity, pressure, 0)
    cell_speed = jnp.abs(velocity[0]) + sound_speed
    face_flux = rusanov(extended[:, :-1], extended[:, 1:], cell_flux[:, :-1], cell_flux[:, 1:], cell_speed[:-1], cell_speed[1:])
    interior = extended[:, 1:-1]
    change = face_flux[:, 1:] - face_flux[:, :-1]
    inner_velocity = velocity[:, 1:-1]
    inner_pressure = pressure[1:-1]
    inner_sound = sound_speed[1:-1]
    for normal in (1, 2):
        side_flux = physical_flux(interior, inner_velocity, inner_pressure, normal)
        side_speed = jnp.abs(inner_velocity[normal]) + inner_sound
        grid_axis = normal + 1
        face_values = rusanov(interior, jnp.roll(interior, -1, grid_axis), side_flux, jnp.roll(side_flux, -1, grid_axis), side_speed, jnp.roll(side_speed, -1, normal))
        change = change + (face_values - jnp.roll(face_values, 1, grid_axis))
    return (interior - time_step * change, face_flux)

def patch_step(inputs):
    fine_patch, ghosts = inputs
    updated = fine_patch
    face_low = jnp.zeros((FIELDS, FY, FZ), jnp.float32)
    face_high = jnp.zeros((FIELDS, FY, FZ), jnp.float32)
    for substep in range(SUBSTEPS):
        time_frac = 0.5 * substep
        ghost_low = (1.0 - time_frac) * ghosts[0, 0] + time_frac * ghosts[1, 0]
        ghost_high = (1.0 - time_frac) * ghosts[0, 1] + time_frac * ghosts[1, 1]
        extended = jnp.concatenate([ghost_low[:, None], updated, ghost_high[:, None]], axis=1)
        updated, face_flux = advance(extended)
        face_low = face_low + face_flux[:, 0]
        face_high = face_high + face_flux[:, -1]
    return (updated, face_low, face_high)

def reference(fine_state, patch_ghosts, coarse_state, coarse_face_term, dest_grp, dest_column):
    fine_new, face_low, face_high = lax.map(patch_step, (fine_state, patch_ghosts))
    averaged = fine_new.reshape(N_GRP, FIELDS, NXF // 2, 2, FY // 2, 2, CZ, 2).mean(axis=(3, 5, 7))
    averaged = averaged.reshape(N_GRP, FIELDS, N_BOX, FX // 2, FY // 2, CZ)
    avg_records = averaged.transpose(0, 2, 3, 4, 1, 5).reshape(N_GRP, N_BOX, NCOL, FIELDS, CZ)
    low_sum = face_low.reshape(N_GRP, FIELDS, FY // 2, 2, CZ, 2).sum(axis=(3, 5)).transpose(0, 2, 1, 3)
    high_sum = face_high.reshape(N_GRP, FIELDS, FY // 2, 2, CZ, 2).sum(axis=(3, 5)).transpose(0, 2, 1, 3)
    low_term = -time_step / 8 * low_sum
    high_term = time_step / 8 * high_sum
    box_ids = jnp.arange(N_BOX, dtype=jnp.int32)[None, :, None, None, None]
    flux_records = jnp.where(box_ids == 0, low_term[:, None], jnp.where(box_ids == N_BOX - 1, high_term[:, None], 0.0))
    payload = jnp.concatenate([avg_records, flux_records], axis=2)
    record_ids = jnp.arange(REC, dtype=jnp.int32)[None, None, :]
    box_index = jnp.broadcast_to(jnp.arange(N_BOX, dtype=jnp.int32)[None, :, None], (N_GRP, N_BOX, REC))
    is_average = jnp.broadcast_to(record_ids < NCOL, (N_GRP, N_BOX, REC))
    end_box = (box_index == 0) | (box_index == N_BOX - 1)
    is_face = (record_ids >= NCOL) & end_box
    is_live = is_average | is_face
    values = jnp.zeros((N_GRP, N_BOX, REC, FIELDS, CZ), jnp.float32).at[dest_grp, box_index, dest_column].add(jnp.where(is_live[..., None, None], payload, 0.0))
    avg_flag = jnp.zeros((N_GRP, N_BOX, REC), jnp.float32).at[dest_grp, box_index, dest_column].add(is_average.astype(jnp.float32))
    face_flag = jnp.zeros((N_GRP, N_BOX, REC), jnp.float32).at[dest_grp, box_index, dest_column].add(is_face.astype(jnp.float32))
    coarse_new = jnp.where(avg_flag[..., None, None] > 0, values, coarse_state + face_flag[..., None, None] * (values - coarse_face_term))
    return (fine_new, coarse_new)
```

```python
import functools

import jax
import jax.numpy as jnp
from jax import lax
from jax.experimental import pallas as pl
from jax.experimental.pallas import tpu as pltpu
from jax.sharding import PartitionSpec as P

MESH = pl.DeviceIdType.MESH
HALF_STEP = 0.03
NX, NZ, NB = 4, 16, 8
F = 5


def primitives(u):
    inverse = 1.0 / u[0]
    v = [u[1] * inverse, u[2] * inverse, u[3] * inverse]
    kinetic = 0.5 * (u[1] * v[0] + u[2] * v[1] + u[3] * v[2])
    pressure = 0.4 * (u[4] - kinetic)
    sound = jnp.sqrt(1.4 * pressure * inverse)
    return v + [pressure, sound]


def flux(u, q, d):
    out = [u[1 + d]]
    for m in range(3):
        f = u[1 + m] * q[d]
        out.append(f + q[3] if m == d else f)
    out.append((u[4] + q[3]) * q[d])
    return out


def kernel(
    fine, ghosts, state, term, dgrp, dcol,
    fine_out, coarse_out,
    ext, mid, q1, q2, fx, fnew, gbuf, face_sum, sums, rec, slots, recv,
    code_tx, code_rx, idx_v, state_v, term_v, coarse_v,
    dg_s, dc_s, inv_s, src_s,
    in_sem, halo_s, halo_r, code_s, code_r, rec_s, rec_r,
):
    me = lax.axis_index("grp")
    box = lax.axis_index("box")
    at_low = box == 0
    at_high = box == NB - 1
    mx, mz = lax.div(me, NZ), lax.rem(me, NZ)

    offsets = [(dx, dz) for dx in range(NX) for dz in range(NZ) if (dx, dz) != (0, 0)]
    offsets.sort(key=lambda o: -(min(o[0], NX - o[0]) + min(o[1], NZ - o[1])))

    def peer(o):
        return lax.rem(mx + o[0], NX) * NZ + lax.rem(mz + o[1], NZ)

    barrier = pltpu.get_barrier_semaphore()
    for o in offsets:
        pl.semaphore_signal(barrier, inc=1, device_id={"grp": peer(o)}, device_id_type=MESH)

    @pl.when(jnp.logical_not(at_low))
    def _():
        pl.semaphore_signal(barrier, inc=1, device_id={"box": box - 1}, device_id_type=MESH)

    @pl.when(jnp.logical_not(at_high))
    def _():
        pl.semaphore_signal(barrier, inc=1, device_id={"box": box + 1}, device_id_type=MESH)

    load_fine = pltpu.make_async_copy(fine.at[0], ext.at[:, pl.ds(2, 4)], in_sem.at[0])
    load_dg = pltpu.make_async_copy(dgrp, dg_s, in_sem.at[1])
    load_dc = pltpu.make_async_copy(dcol, dc_s, in_sem.at[2])
    load_state = pltpu.make_async_copy(state.at[0, 0], state_v, in_sem.at[3])
    load_term = pltpu.make_async_copy(term.at[0, 0], term_v, in_sem.at[4])
    load_dg.start()
    load_dc.start()
    load_fine.start()

    def ghost_loads(side):
        near, far = (1, 0) if side == 0 else (6, 7)
        return [
            pltpu.make_async_copy(ghosts.at[0, 0, side], ext.at[:, near], in_sem.at[5]),
            pltpu.make_async_copy(ghosts.at[0, 0, side], ext.at[:, far], in_sem.at[6]),
            pltpu.make_async_copy(ghosts.at[0, 1, side], gbuf, in_sem.at[7]),
        ]

    @pl.when(at_low)
    def _():
        for c in ghost_loads(0):
            c.start()

    @pl.when(at_high)
    def _():
        for c in ghost_loads(1):
            c.start()

    load_state.start()
    load_term.start()

    lane = lax.broadcasted_iota(jnp.int32, (1, 128), 1)
    load_dg.wait()
    load_dc.wait()
    live_face = jnp.where(at_low | at_high, 1, 0)
    which = jnp.full((1, 128), 24, jnp.int32)
    code = jnp.zeros((1, 128), jnp.int32)
    for r in range(24):
        hit = lane == dg_s[0, 0, r]
        which = jnp.where(hit, r, which)
        value = dc_s[0, 0, r] + 1
        if r >= 16:
            value = (value + 32) * live_face
        code = jnp.where(hit, value, code)
    code_tx[...] = code.astype(jnp.float32)
    idx_v[0] = which
    to_inv = pltpu.make_async_copy(idx_v.at[0], inv_s, in_sem.at[8])
    to_inv.start()

    load_fine.wait()
    neighbours = jnp.where(at_low | at_high, 1, 2)
    pl.semaphore_wait(barrier, 63 + neighbours)

    def halo_down():
        return pltpu.make_async_remote_copy(
            ext.at[:, pl.ds(2, 2)], ext.at[:, pl.ds(6, 2)], halo_s.at[0], halo_r.at[0],
            device_id={"box": box - 1}, device_id_type=MESH,
        )

    def halo_up():
        return pltpu.make_async_remote_copy(
            ext.at[:, pl.ds(4, 2)], ext.at[:, pl.ds(0, 2)], halo_s.at[1], halo_r.at[1],
            device_id={"box": box + 1}, device_id_type=MESH,
        )

    @pl.when(jnp.logical_not(at_low))
    def _():
        halo_down().start()

    @pl.when(jnp.logical_not(at_high))
    def _():
        halo_up().start()

    def code_copy(o):
        p = peer(o)
        return pltpu.make_async_remote_copy(
            code_tx, code_rx.at[me], code_s, code_r, device_id={"grp": p}, device_id_type=MESH
        )

    for o in offsets:
        code_copy(o).start()
    code_rx[me] = code_tx[...]

    def prim_plane(u_ref, q_ref, i):
        q = primitives([u_ref[f, i] for f in range(F)])
        for f in range(F):
            q_ref[f, i] = q[f]

    def face_plane(u_ref, q_ref, i):
        ul, ur = [u_ref[f, i] for f in range(F)], [u_ref[f, i + 1] for f in range(F)]
        ql, qr = [q_ref[f, i] for f in range(F)], [q_ref[f, i + 1] for f in range(F)]
        fl, fr = flux(ul, ql, 0), flux(ur, qr, 0)
        biggest = jnp.maximum(jnp.abs(ql[0]) + ql[4], jnp.abs(qr[0]) + qr[4])
        for f in range(F):
            fx[f, i] = (fl[f] + fr[f]) - biggest * (ur[f] - ul[f])

    def update_plane(u_ref, q_ref, i, dst, j):
        u = [u_ref[f, i] for f in range(F)]
        q = [q_ref[f, i] for f in range(F)]
        change = [fx[f, i] - fx[f, i - 1] for f in range(F)]
        for d, axis, size in ((1, 0, 16), (2, 1, 256)):
            fl = flux(u, q, d)
            s = jnp.abs(q[d]) + q[4]
            biggest = jnp.maximum(s, pltpu.roll(s, size - 1, axis))
            for f in range(F):
                up, fp = pltpu.roll(u[f], size - 1, axis), pltpu.roll(fl[f], size - 1, axis)
                face = (fl[f] + fp) - biggest * (up - u[f])
                change[f] = change[f] + (face - pltpu.roll(face, 1, axis))
        for f in range(F):
            dst[f, j] = u[f] - HALF_STEP * change[f]

    def loop(lo, hi, body):
        def step(i, carry):
            body(i)
            return carry

        lax.fori_loop(lo, hi, step, 0)

    loop(2, 6, lambda i: prim_plane(ext, q1, i))
    loop(2, 5, lambda i: face_plane(ext, q1, i))
    loop(3, 5, lambda i: update_plane(ext, q1, i, mid, i))

    @pl.when(jnp.logical_not(at_low))
    def _():
        halo_down().wait_send()
        halo_up().wait_recv()

    @pl.when(at_low)
    def _():
        for c in ghost_loads(0):
            c.wait()

    @pl.when(jnp.logical_not(at_high))
    def _():
        halo_up().wait_send()
        halo_down().wait_recv()

    @pl.when(at_high)
    def _():
        for c in ghost_loads(1):
            c.wait()

    loop(0, 2, lambda i: prim_plane(ext, q1, i))
    loop(6, 8, lambda i: prim_plane(ext, q1, i))
    loop(0, 2, lambda i: face_plane(ext, q1, i))
    loop(5, 7, lambda i: face_plane(ext, q1, i))
    loop(1, 3, lambda i: update_plane(ext, q1, i, mid, i))
    loop(5, 7, lambda i: update_plane(ext, q1, i, mid, i))

    scale = jnp.where(at_low, -0.0075 * 0.5, 0.0075 * 0.5)
    edge = jnp.where(at_low, 1, 5)
    for f in range(F):
        face_sum[f] = fx[f, edge]

    @pl.when(at_low)
    def _():
        for f in range(F):
            mid[f, 1] = 0.5 * ext[f, 1] + 0.5 * gbuf[f]

    @pl.when(at_high)
    def _():
        for f in range(F):
            mid[f, 6] = 0.5 * ext[f, 6] + 0.5 * gbuf[f]

    loop(1, 7, lambda i: prim_plane(mid, q2, i))
    loop(1, 6, lambda i: face_plane(mid, q2, i))
    loop(2, 6, lambda i: update_plane(mid, q2, i, fnew, i - 2))
    store_fine = pltpu.make_async_copy(fnew, fine_out.at[0], in_sem.at[0])
    store_fine.start()

    def put(k, value):
        for h in range(2):
            sums[k, h] = value[:, 128 * h : 128 * (h + 1)]

    for f in range(F):
        put(3 * f + 2, scale * (face_sum[f] + fx[f, edge]))
        for r in range(2):
            put(3 * f + r, 0.125 * (fnew[f, 2 * r] + fnew[f, 2 * r + 1]))
    rows = lax.broadcasted_iota(jnp.int32, (256, 128), 0)
    cols = lax.broadcasted_iota(jnp.int32, (256, 128), 1)
    pairs = jnp.where(lax.shift_right_logical(rows, 1) == cols, 1.0, 0.0).astype(jnp.float32)
    coarse = jnp.zeros((120, 128), jnp.float32)
    for h in range(2):
        rows_h = [
            sums[k, h, pl.ds(0, 8, stride=2), :] + sums[k, h, pl.ds(1, 8, stride=2), :]
            for k in range(15)
        ]
        coarse = coarse + jnp.dot(
            jnp.concatenate(rows_h, axis=0),
            pairs[128 * h : 128 * (h + 1)],
            precision=lax.Precision.HIGHEST,
            preferred_element_type=jnp.float32,
        )
    for f in range(F):
        for r in range(3):
            for k in range(8):
                at = (3 * f + r) * 8 + k
                rec[8 * r + k, pl.ds(f, 1), :] = coarse[at : at + 1]
    rec[24] = jnp.zeros((F, 128), jnp.float32)

    to_inv.wait()

    def fill(s, carry):
        slots[s] = rec[inv_s[0, s]]
        return carry

    lax.fori_loop(0, 64, fill, 0, unroll=8)

    for o in offsets:
        p = peer(o)
        pltpu.make_async_remote_copy(
            slots.at[p], recv.at[me], rec_s, rec_r, device_id={"grp": p}, device_id_type=MESH
        ).start()
    recv[me] = slots[me]

    def totals(buffer, send, receive):
        return pltpu.make_async_remote_copy(
            buffer.at[pl.ds(0, 63)], buffer.at[pl.ds(0, 63)], send, receive,
            device_id={"grp": peer((1, 0))}, device_id_type=MESH,
        )

    totals(code_rx, code_s, code_r).wait()
    target = (lane + 1).astype(jnp.float32)
    mine = lane == me

    def decode(s, carry):
        src, kind = carry
        value = jnp.sum(jnp.where(mine, code_rx[s], 0.0), axis=1, keepdims=True)
        average = value == target
        face = value == target + 32.0
        return (
            jnp.where(average | face, s, src),
            jnp.where(average, 1, jnp.where(face, 2, kind)),
        )

    zero = jnp.zeros((1, 128), jnp.int32)
    src, kind = lax.fori_loop(0, 64, decode, (zero, zero), unroll=8)
    idx_v[0] = src
    idx_v[1] = kind
    to_src = pltpu.make_async_copy(idx_v, src_s, in_sem.at[8])
    to_src.start()
    load_state.wait()
    load_term.wait()
    to_src.wait()

    totals(recv, rec_s, rec_r).wait()

    def combine(c, carry):
        value = recv[src_s[0, 0, c]]
        kind = src_s[1, 0, c]
        base = state_v[c]
        coarse_v[c] = jnp.where(
            kind == 1, value, jnp.where(kind == 2, base + value - term_v[c], base)
        )
        return carry

    lax.fori_loop(0, 24, combine, 0, unroll=8)
    store_coarse = pltpu.make_async_copy(coarse_v, coarse_out.at[0, 0], in_sem.at[1])
    store_coarse.start()
    store_fine.wait()
    store_coarse.wait()


def on_device(fine_state, patch_ghosts, coarse_state, coarse_face_term, dest_grp, dest_column):
    any_spec = pl.BlockSpec(memory_space=pl.ANY)
    vm, f32 = pltpu.VMEM, jnp.float32
    dma = pltpu.SemaphoreType.DMA
    return pl.pallas_call(
        kernel,
        out_shape=(
            jax.ShapeDtypeStruct(fine_state.shape, f32),
            jax.ShapeDtypeStruct(coarse_state.shape, f32),
        ),
        in_specs=[any_spec] * 6,
        out_specs=(any_spec, any_spec),
        scratch_shapes=[
            vm((F, 8, 16, 256), f32),
            vm((F, 8, 16, 256), f32),
            vm((F, 8, 16, 256), f32),
            vm((F, 8, 16, 256), f32),
            vm((F, 8, 16, 256), f32),
            vm((F, 4, 16, 256), f32),
            vm((F, 16, 256), f32),
            vm((F, 16, 256), f32),
            vm((15, 2, 16, 128), f32),
            vm((25, F, 128), f32),
            vm((64, F, 128), f32),
            vm((64, F, 128), f32),
            vm((1, 128), f32),
            vm((64, 1, 128), f32),
            vm((2, 1, 128), jnp.int32),
            vm((24, F, 128), f32),
            vm((24, F, 128), f32),
            vm((24, F, 128), f32),
            pltpu.SMEM((1, 1, 24), jnp.int32),
            pltpu.SMEM((1, 1, 24), jnp.int32),
            pltpu.SMEM((1, 128), jnp.int32),
            pltpu.SMEM((2, 1, 128), jnp.int32),
            dma((9,)),
            dma((2,)),
            dma((2,)),
            dma,
            dma,
            dma,
            dma,
        ],
        compiler_params=pltpu.CompilerParams(collective_id=0, has_side_effects=True),
    )(fine_state, patch_ghosts, coarse_state, coarse_face_term, dest_grp, dest_column)


def solution(mesh):
    in_specs = (
        P("grp", None, "box", None, None),
        P("grp", None, None, None, None, None),
        P("grp", "box", None, None, None),
        P("grp", "box", None, None, None),
        P("grp", "box", None),
        P("grp", "box", None),
    )
    out_specs = (P("grp", None, "box", None, None), P("grp", "box", None, None, None))
    return jax.shard_map(
        on_device, mesh=mesh, in_specs=in_specs, out_specs=out_specs, check_vma=False
    )
```

```python
import jax
import jax.numpy as jnp
from jax import lax
from jax.experimental import pallas as pl
from jax.experimental.pallas import tpu as pltpu
from jax.sharding import PartitionSpec as P

MESH = pl.DeviceIdType.MESH
HALF_STEP = 0.03
NX, NZ, NB = 4, 16, 8
F, REC, NAVG, CZ = 5, 24, 16, 128


def primitives(u):
    inverse = 1.0 / u[0]
    v = [u[1] * inverse, u[2] * inverse, u[3] * inverse]
    kinetic = 0.5 * (u[1] * v[0] + u[2] * v[1] + u[3] * v[2])
    pressure = 0.4 * (u[4] - kinetic)
    sound = jnp.sqrt(1.4 * pressure * inverse)
    return v + [pressure, sound]


def flux(u, q, d):
    out = [u[1 + d]]
    for m in range(3):
        f = u[1 + m] * q[d]
        out.append(f + q[3] if m == d else f)
    out.append((u[4] + q[3]) * q[d])
    return out


def kernel(
    fine, ghosts, state, term, dgrp, dcol,
    fnew, coarse_out,
    ext, mid, q1, q2, fx, gbuf, face_sum, sums, rec, slots, recv, gathered,
    code_tx, code_x, bundle, code_z, table, found, state_v, term_v,
    dg_s, dc_s, inv_s, src_s,
    in_sem, halo_s, halo_r, cx_s, cx_r, cz_s, cz_r, rec_s, rec_r, hello,
):
    me = lax.axis_index("grp")
    box = lax.axis_index("box")
    at_low = box == 0
    at_high = box == NB - 1
    mx, mz = lax.div(me, NZ), lax.rem(me, NZ)

    def peer(dx, dz):
        return lax.rem(mx + dx, NX) * NZ + lax.rem(mz + dz, NZ)

    def signal(sem, **where):
        pl.semaphore_signal(sem, inc=1, device_id=where, device_id_type=MESH)

    def greet(sem, steps):
        for dx, dz in steps:
            signal(sem, grp=peer(dx, dz))

    barrier = pltpu.get_barrier_semaphore()

    @pl.when(jnp.logical_not(at_low))
    def _():
        signal(barrier, box=box - 1)

    @pl.when(jnp.logical_not(at_high))
    def _():
        signal(barrier, box=box + 1)

    rows = [(dx, 0) for dx in range(1, NX)]
    greet(barrier, [(0, 1), (0, NZ - 1)] + rows)

    def local(src, dst, at):
        return pltpu.make_async_copy(src, dst, in_sem.at[at])

    load_fine = local(fine.at[0], ext.at[:, pl.ds(2, 4)], 0)
    load_dg = local(dgrp, dg_s, 1)
    load_dc = local(dcol, dc_s, 2)
    load_state = local(state, state_v, 3)
    load_term = local(term, term_v, 4)
    load_fine.start()
    load_dg.start()
    load_dc.start()

    def ghost_loads(side):
        near, far = (1, 0) if side == 0 else (6, 7)
        return [
            local(ghosts.at[0, 0, side], ext.at[:, near], 5),
            local(ghosts.at[0, 0, side], ext.at[:, far], 6),
            local(ghosts.at[0, 1, side], gbuf, 7),
        ]

    @pl.when(at_low)
    def _():
        for c in ghost_loads(0):
            c.start()

    @pl.when(at_high)
    def _():
        for c in ghost_loads(1):
            c.start()

    load_state.start()
    load_term.start()

    lane = lax.broadcasted_iota(jnp.int32, (1, 128), 1)
    load_dg.wait()
    load_dc.wait()
    live_face = jnp.where(at_low | at_high, 1, 0)
    which = jnp.full((1, 128), REC, jnp.int32)
    code = jnp.zeros((1, 128), jnp.int32)
    for r in range(REC):
        hit = lane == dg_s[0, 0, r]
        which = jnp.where(hit, r, which)
        value = dc_s[0, 0, r] + 1
        if r >= NAVG:
            value = (value + 32) * live_face
        code = jnp.where(hit, value, code)
    code_tx[...] = code.astype(jnp.float32)
    table[...] = which
    to_inv = local(table, inv_s, 8)
    to_inv.start()

    load_fine.wait()
    pl.semaphore_wait(barrier, NX + 1 + jnp.where(at_low | at_high, 1, 2))

    def halo_down():
        return pltpu.make_async_remote_copy(
            ext.at[:, pl.ds(2, 2)], ext.at[:, pl.ds(6, 2)], halo_s.at[0], halo_r.at[0],
            device_id={"box": box - 1}, device_id_type=MESH,
        )

    def halo_up():
        return pltpu.make_async_remote_copy(
            ext.at[:, pl.ds(4, 2)], ext.at[:, pl.ds(0, 2)], halo_s.at[1], halo_r.at[1],
            device_id={"box": box + 1}, device_id_type=MESH,
        )

    @pl.when(jnp.logical_not(at_low))
    def _():
        halo_down().start()

    @pl.when(jnp.logical_not(at_high))
    def _():
        halo_up().start()

    greet(hello.at[0], [(0, 1), (0, NZ - 1)])

    def send(src, dst, s, r, to):
        return pltpu.make_async_remote_copy(
            src, dst, s, r, device_id={"grp": to}, device_id_type=MESH
        )

    for dx in range(1, NX):
        send(code_tx, code_x.at[mx], cx_s, cx_r, peer(dx, 0)).start()
    code_x[mx] = code_tx[...]

    def prim_plane(u_ref, q_ref, i):
        q = primitives([u_ref[f, i] for f in range(F)])
        for f in range(F):
            q_ref[f, i] = q[f]

    def face_plane(u_ref, q_ref, i):
        ul, ur = [u_ref[f, i] for f in range(F)], [u_ref[f, i + 1] for f in range(F)]
        ql, qr = [q_ref[f, i] for f in range(F)], [q_ref[f, i + 1] for f in range(F)]
        fl, fr = flux(ul, ql, 0), flux(ur, qr, 0)
        biggest = jnp.maximum(jnp.abs(ql[0]) + ql[4], jnp.abs(qr[0]) + qr[4])
        for f in range(F):
            fx[f, i] = (fl[f] + fr[f]) - biggest * (ur[f] - ul[f])

    def update_plane(u_ref, q_ref, i, dst, j):
        u = [u_ref[f, i] for f in range(F)]
        q = [q_ref[f, i] for f in range(F)]
        change = [fx[f, i] - fx[f, i - 1] for f in range(F)]
        for d, axis, size in ((1, 0, 16), (2, 1, 256)):
            fl = flux(u, q, d)
            s = jnp.abs(q[d]) + q[4]
            biggest = jnp.maximum(s, pltpu.roll(s, size - 1, axis))
            for f in range(F):
                up, fp = pltpu.roll(u[f], size - 1, axis), pltpu.roll(fl[f], size - 1, axis)
                face = (fl[f] + fp) - biggest * (up - u[f])
                change[f] = change[f] + (face - pltpu.roll(face, 1, axis))
        for f in range(F):
            dst[f, j] = u[f] - HALF_STEP * change[f]

    def loop(start, count, body):
        def step(i, carry):
            body(start + i)
            return carry

        lax.fori_loop(0, count, step, 0)

    loop(2, 4, lambda i: prim_plane(ext, q1, i))
    pl.semaphore_wait(hello.at[0], 2)
    greet(hello.at[1], [(0, 2), (0, NZ - 2)])
    loop(2, 3, lambda i: face_plane(ext, q1, i))
    loop(3, 2, lambda i: update_plane(ext, q1, i, mid, i))

    def row_total(buffer, count, s, r):
        return send(buffer.at[pl.ds(0, count)], buffer.at[pl.ds(0, count)], s, r, peer(0, 1))

    row_total(code_x, NX - 1, cx_s, cx_r).wait()
    packed = jnp.zeros((1, 128), jnp.float32)
    for sx in range(NX):
        moved = pltpu.roll(code_x[sx], lax.rem(128 + (sx - mx) * NZ, 128), 1)
        packed = jnp.where((lane >= sx * NZ) & (lane < (sx + 1) * NZ), moved, packed)
    bundle[...] = packed
    code_z[mz] = packed

    def side(low):
        p, e, u = (jnp.where(low, 0, 6), jnp.where(low, 0, 5), jnp.where(low, 1, 5))
        loop(p, 2, lambda i: prim_plane(ext, q1, i))
        loop(e, 2, lambda i: face_plane(ext, q1, i))
        loop(u, 2, lambda i: update_plane(ext, q1, i, mid, i))

    def wait_low():
        @pl.when(jnp.logical_not(at_low))
        def _():
            halo_down().wait_send()
            halo_up().wait_recv()

        @pl.when(at_low)
        def _():
            for c in ghost_loads(0):
                c.wait()

    def wait_high():
        @pl.when(jnp.logical_not(at_high))
        def _():
            halo_up().wait_send()
            halo_down().wait_recv()

        @pl.when(at_high)
        def _():
            for c in ghost_loads(1):
                c.wait()

    odd = lax.rem(box, 2) == 1
    even = jnp.logical_not(odd)

    @pl.when(odd)
    def _():
        wait_low()

    @pl.when(even)
    def _():
        wait_high()

    side(odd)
    pl.semaphore_wait(hello.at[1], 2)
    greet(hello.at[2], [(0, 4), (0, NZ - 4)])

    @pl.when(odd)
    def _():
        wait_high()

    @pl.when(even)
    def _():
        wait_low()

    side(even)

    scale = jnp.where(at_low, -0.0075 * 0.5, 0.0075 * 0.5)
    edge = jnp.where(at_low, 1, 5)
    for f in range(F):
        face_sum[f] = fx[f, edge]

    @pl.when(at_low)
    def _():
        for f in range(F):
            mid[f, 1] = 0.5 * ext[f, 1] + 0.5 * gbuf[f]

    @pl.when(at_high)
    def _():
        for f in range(F):
            mid[f, 6] = 0.5 * ext[f, 6] + 0.5 * gbuf[f]

    loop(1, 6, lambda i: prim_plane(mid, q2, i))
    loop(1, 5, lambda i: face_plane(mid, q2, i))
    loop(2, 4, lambda i: update_plane(mid, q2, i, fnew, i - 2))

    def put(k, value):
        for h in range(2):
            sums[k, h] = value[:, 128 * h : 128 * (h + 1)]

    for f in range(F):
        put(3 * f + 2, scale * (face_sum[f] + fx[f, edge]))
        for r in range(2):
            put(3 * f + r, 0.125 * (fnew[f, 2 * r] + fnew[f, 2 * r + 1]))
    fine_z = lax.broadcasted_iota(jnp.int32, (256, CZ), 0)
    coarse_z = lax.broadcasted_iota(jnp.int32, (256, CZ), 1)
    pairs = jnp.where(lax.shift_right_logical(fine_z, 1) == coarse_z, 1.0, 0.0).astype(jnp.float32)
    coarse = jnp.zeros((3 * F * 8, CZ), jnp.float32)
    for h in range(2):
        part = [
            sums[k, h, pl.ds(0, 8, stride=2), :] + sums[k, h, pl.ds(1, 8, stride=2), :]
            for k in range(3 * F)
        ]
        coarse = coarse + jnp.dot(
            jnp.concatenate(part, axis=0),
            pairs[128 * h : 128 * (h + 1)],
            precision=lax.Precision.HIGHEST,
            preferred_element_type=jnp.float32,
        )
    for f in range(F):
        for r in range(3):
            for k in range(8):
                at = (3 * f + r) * 8 + k
                rec[8 * r + k, pl.ds(f, 1), :] = coarse[at : at + 1]
    rec[REC] = jnp.zeros((F, CZ), jnp.float32)

    pl.semaphore_wait(hello.at[2], 2)
    greet(hello.at[3], rows)
    to_inv.wait()

    def fill(s, carry):
        slots[s] = rec[jnp.clip(inv_s[0, s], 0, REC)]
        return carry

    lax.fori_loop(0, NX * NZ, fill, 0, unroll=8)

    def send_rows(steps):
        for dz in steps:
            for dx in (2, 1, 3, 0):
                if (dx, dz) != (0, 0):
                    to = peer(dx, dz)
                    send(slots.at[to], recv.at[me], rec_s, rec_r, to).start()

    def send_codes(steps):
        for dz in steps:
            send(bundle, code_z.at[mz], cz_s, cz_r, peer(0, dz)).start()

    send_rows([7, 9, 6, 10])
    pl.semaphore_wait(hello.at[3], NX - 1)
    send_rows([8])
    send_codes([8, 7, 9, 6, 10, 5, 11, 4, 12, 3, 13, 2, 14, 1, 15])
    send_rows([5, 11, 4, 12, 3, 13, 2, 14, 1, 15, 0])
    recv[me] = slots[me]
    recv[NX * NZ] = jnp.zeros((F, CZ), jnp.float32)

    row_total(code_z, NZ - 1, cz_s, cz_r).wait()
    owner_z = lax.bitwise_and(lane, NZ - 1) == mz
    valid = owner_z & (lane < NX * NZ)
    source = lax.bitwise_and(lane, -NZ) + 1
    hits = []
    for c in range(REC):
        hits.append(jnp.zeros((1, 128), jnp.int32))
    for sz in range(NZ):
        codes = jnp.where(valid, code_z[sz].astype(jnp.int32), 0)
        slot = source + sz
        for c in range(REC):
            average, face = codes == c + 1, codes == c + 33
            hits[c] = hits[c] + jnp.where(average, slot, jnp.where(face, slot + 128, 0))
    total = jnp.sum(
        jnp.concatenate(hits, axis=0).astype(jnp.float32), axis=1, keepdims=True
    ).astype(jnp.int32)
    total = jnp.broadcast_to(total, (REC, 128))
    is_face = total > 128
    found[...] = jnp.where(total == 0, NX * NZ, jnp.where(is_face, total - 129, total - 1))
    to_src = local(found, src_s, 8)
    to_src.start()
    load_state.wait()
    load_term.wait()
    for f in range(F):
        base = state_v[f]
        state_v[f] = jnp.where(
            total == 0, base, jnp.where(is_face, base - term_v[f], jnp.zeros_like(base))
        )
    to_src.wait()

    row_total(recv, NX * NZ - 1, rec_s, rec_r).wait()
    for c in range(REC):
        value = recv[jnp.clip(src_s[c, 0], 0, NX * NZ)]
        for f in range(F):
            gathered[f, pl.ds(c, 1), :] = value[f : f + 1]
    for f in range(F):
        coarse_out[f] = state_v[f] + gathered[f]


def store_kernel(fine_v, coarse_v, fine_out, coarse_out, sem):
    copies = [
        pltpu.make_async_copy(fine_v, fine_out.at[0], sem.at[0]),
        pltpu.make_async_copy(coarse_v, coarse_out, sem.at[1]),
    ]
    for c in copies:
        c.start()
    for c in copies:
        c.wait()


def on_device(fine_state, patch_ghosts, coarse_state, coarse_face_term, dest_grp, dest_column):
    any_spec = pl.BlockSpec(memory_space=pl.ANY)
    vmem_spec = pl.BlockSpec(memory_space=pltpu.VMEM)
    vm, sm, f32, i32 = pltpu.VMEM, pltpu.SMEM, jnp.float32, jnp.int32
    dma = pltpu.SemaphoreType.DMA
    fine_new, coarse_new = pl.pallas_call(
        kernel,
        out_shape=(vm((F, 4, 16, 256), f32), vm((F, REC, CZ), f32)),
        in_specs=[any_spec] * 6,
        out_specs=(vmem_spec, vmem_spec),
        scratch_shapes=[
            vm((F, 8, 16, 256), f32),
            vm((F, 8, 16, 256), f32),
            vm((F, 8, 16, 256), f32),
            vm((F, 8, 16, 256), f32),
            vm((F, 8, 16, 256), f32),
            vm((F, 16, 256), f32),
            vm((F, 16, 256), f32),
            vm((3 * F, 2, 16, 128), f32),
            vm((REC + 1, F, CZ), f32),
            vm((NX * NZ, F, CZ), f32),
            vm((NX * NZ + 1, F, CZ), f32),
            vm((F, REC, CZ), f32),
            vm((1, 128), f32),
            vm((NX, 1, 128), f32),
            vm((1, 128), f32),
            vm((NZ, 1, 128), f32),
            vm((1, 128), i32),
            vm((REC, 128), i32),
            vm((F, REC, CZ), f32),
            vm((F, REC, CZ), f32),
            sm((1, 1, REC), i32),
            sm((1, 1, REC), i32),
            sm((1, 128), i32),
            sm((REC, 128), i32),
            dma((9,)),
            dma((2,)),
            dma((2,)),
            dma,
            dma,
            dma,
            dma,
            dma,
            dma,
            pltpu.SemaphoreType.REGULAR((4,)),
        ],
        compiler_params=pltpu.CompilerParams(collective_id=0, has_side_effects=True),
    )(
        fine_state,
        patch_ghosts,
        coarse_state[0, 0].transpose(1, 0, 2),
        coarse_face_term[0, 0].transpose(1, 0, 2),
        dest_grp,
        dest_column,
    )
    fine_new, coarse_new = pl.pallas_call(
        store_kernel,
        out_shape=(
            jax.ShapeDtypeStruct(fine_state.shape, f32),
            jax.ShapeDtypeStruct((F, REC, CZ), f32),
        ),
        in_specs=[vmem_spec] * 2,
        out_specs=(any_spec, any_spec),
        scratch_shapes=[dma((2,))],
    )(
        pltpu.with_memory_space_constraint(fine_new, vm),
        pltpu.with_memory_space_constraint(coarse_new, vm),
    )
    return fine_new, coarse_new.transpose(1, 0, 2)[None, None]


def solution(mesh):
    in_specs = (
        P("grp", None, "box", None, None),
        P("grp", None, None, None, None, None),
        P("grp", "box", None, None, None),
        P("grp", "box", None, None, None),
        P("grp", "box", None),
        P("grp", "box", None),
    )
    out_specs = (P("grp", None, "box", None, None), P("grp", "box", None, None, None))
    return jax.shard_map(
        on_device, mesh=mesh, in_specs=in_specs, out_specs=out_specs, check_vma=False
    )
```

```python
import jax
import jax.numpy as jnp
from jax import lax
from jax.experimental import pallas as pl
from jax.experimental.pallas import tpu as pltpu
from jax.sharding import PartitionSpec as P

MESH = pl.DeviceIdType.MESH
HALF_STEP = 0.03
NX, NZ, NB = 4, 16, 8
F, REC, NAVG, CZ = 5, 24, 16, 128


def primitives(u):
    inverse = 1.0 / u[0]
    v = [u[1] * inverse, u[2] * inverse, u[3] * inverse]
    kinetic = 0.5 * (u[1] * v[0] + u[2] * v[1] + u[3] * v[2])
    pressure = 0.4 * (u[4] - kinetic)
    sound = jnp.sqrt(1.4 * pressure * inverse)
    return v + [pressure, sound]


def flux(u, q, d):
    out = [u[1 + d]]
    for m in range(3):
        f = u[1 + m] * q[d]
        out.append(f + q[3] if m == d else f)
    out.append((u[4] + q[3]) * q[d])
    return out


def face(ul, ur, fl, fr, sl, sr):
    biggest = jnp.maximum(sl, sr)
    return [(fl[f] + fr[f]) - biggest * (ur[f] - ul[f]) for f in range(F)]


def exact_dot(x, to):
    total = None
    for _ in range(3):
        part = x.astype(jnp.bfloat16)
        x = x - part.astype(jnp.float32)
        moved = jnp.dot(part, to, preferred_element_type=jnp.float32)
        total = moved if total is None else total + moved
    return total


def turned(a, axis, shift):
    return pltpu.roll(a, shift % (8, 128)[axis], axis)


def kernel(
    fine, ghosts, state, term, dgrp, dcol,
    fine_out, coarse_out,
    raw, graw, ext, mid, q1, q2, fx, fnew, gbuf, face_sum, rec, slots, recv, gathered,
    code_tx, code_x, bundle, code_z, table, found, state_v, term_v,
    dg_s, dc_s, inv_s, src_s,
    in_sem, halo_s, halo_r, cx_s, cx_r, cz_s, cz_r, rec_s, rec_r, hello,
):
    me = lax.axis_index("grp")
    box = lax.axis_index("box")
    at_low = box == 0
    at_high = box == NB - 1
    mx, mz = lax.div(me, NZ), lax.rem(me, NZ)

    def peer(dx, dz):
        return lax.rem(mx + dx, NX) * NZ + lax.rem(mz + dz, NZ)

    def signal(sem, **where):
        pl.semaphore_signal(sem, inc=1, device_id=where, device_id_type=MESH)

    def greet(sem, steps):
        for dz in steps:
            signal(sem, grp=peer(0, dz))
            signal(sem, grp=peer(0, NZ - dz))

    barrier = pltpu.get_barrier_semaphore()

    @pl.when(jnp.logical_not(at_low))
    def _():
        signal(barrier, box=box - 1)

    @pl.when(jnp.logical_not(at_high))
    def _():
        signal(barrier, box=box + 1)

    greet(barrier, [1, 2])
    for dx in range(1, NX):
        signal(barrier, grp=peer(dx, 0))

    def local(src, dst, at):
        return pltpu.make_async_copy(src, dst, in_sem.at[at])

    def halves(src, dst, at):
        return [
            local(src.at[:, :, pl.ds(128 * h, 128)], dst.at[:, h], at + h) for h in (0, 1)
        ]

    load_fine = [
        local(fine.at[0, :, :, :, pl.ds(128 * h, 128)], raw.at[:, :, h], h) for h in (0, 1)
    ]
    load_dg = local(dgrp, dg_s, 2)
    load_dc = local(dcol, dc_s, 3)
    load_state = local(state, state_v, 4)
    load_term = local(term, term_v, 5)
    for c in load_fine:
        c.start()
    load_dg.start()
    load_dc.start()

    def ghost_loads(end):
        return [c for t in (0, 1) for c in halves(ghosts.at[0, t, end], graw.at[t], 6 + 2 * t)]

    @pl.when(at_low)
    def _():
        for c in ghost_loads(0):
            c.start()

    @pl.when(at_high)
    def _():
        for c in ghost_loads(1):
            c.start()

    load_state.start()
    load_term.start()

    lane = lax.broadcasted_iota(jnp.int32, (1, 128), 1)
    load_dg.wait()
    load_dc.wait()
    live_face = jnp.where(at_low | at_high, 1, 0)
    which = jnp.full((1, 128), REC, jnp.int32)
    code = jnp.zeros((1, 128), jnp.int32)
    for r in range(REC):
        hit = lane == dg_s[0, 0, r]
        which = jnp.where(hit, r, which)
        value = dc_s[0, 0, r] + 1
        if r >= NAVG:
            value = (value + 32) * live_face
        code = jnp.where(hit, value, code)
    code_tx[...] = code.astype(jnp.float32)
    table[...] = which
    to_inv = local(table, inv_s, 10)
    to_inv.start()

    row = lax.broadcasted_iota(jnp.int32, (256, 256), 0)
    col = lax.broadcasted_iota(jnp.int32, (256, 256), 1)

    def cell(split):
        return 2 * lax.bitwise_and(split, 127) + lax.shift_right_logical(split, 7)

    to_split = jnp.where(row == cell(col), 1.0, 0.0).astype(jnp.bfloat16)

    def split_plane(lines, put):
        moved = exact_dot(jnp.concatenate(lines, axis=0), to_split)
        for f in range(F):
            for py in (0, 1):
                at = 8 * (2 * f + py)
                for pz in (0, 1):
                    put(f, 2 * py + pz, moved[at : at + 8, 128 * pz : 128 * (pz + 1)])

    def loop(start, count, body, unroll=1):
        def step(i, carry):
            body(start + i)
            return carry

        lax.fori_loop(0, count, step, 0, unroll=unroll)

    for c in load_fine:
        c.wait()

    def split_fine(i):
        lines = [
            jnp.concatenate([raw[f, i, h, pl.ds(py, 8, stride=2), :] for h in (0, 1)], axis=1)
            for f in range(F)
            for py in (0, 1)
        ]

        def put(f, k, value):
            ext[f, i + 2, k] = value

        split_plane(lines, put)

    loop(0, 4, split_fine, 4)

    pl.semaphore_wait(barrier, NX + 3 + jnp.where(at_low | at_high, 1, 2))

    def halo_down():
        return pltpu.make_async_remote_copy(
            ext.at[:, pl.ds(2, 2)], ext.at[:, pl.ds(6, 2)], halo_s.at[0], halo_r.at[0],
            device_id={"box": box - 1}, device_id_type=MESH,
        )

    def halo_up():
        return pltpu.make_async_remote_copy(
            ext.at[:, pl.ds(4, 2)], ext.at[:, pl.ds(0, 2)], halo_s.at[1], halo_r.at[1],
            device_id={"box": box + 1}, device_id_type=MESH,
        )

    @pl.when(jnp.logical_not(at_low))
    def _():
        halo_down().start()

    @pl.when(jnp.logical_not(at_high))
    def _():
        halo_up().start()

    greet(hello.at[0], [1, 2])

    def send(src, dst, s, r, to):
        return pltpu.make_async_remote_copy(
            src, dst, s, r, device_id={"grp": to}, device_id_type=MESH
        )

    for dx in range(1, NX):
        send(code_tx, code_x.at[mx], cx_s, cx_r, peer(dx, 0)).start()
    code_x[mx] = code_tx[...]

    def prim_plane(u_ref, q_ref, i):
        for k in range(4):
            q = primitives([u_ref[f, i, k] for f in range(F)])
            for f in range(F):
                q_ref[f, i, k] = q[f]

    def sides(u_ref, q_ref, places, d):
        out = []
        for i, k in places:
            u, q = [[ref[f, i, k] for f in range(F)] for ref in (u_ref, q_ref)]
            out.append((u, flux(u, q, d), jnp.abs(q[d]) + q[4]))
        return out

    def face_plane(u_ref, q_ref, i):
        for k in range(4):
            (ul, fl, sl), (ur, fr, sr) = sides(u_ref, q_ref, ((i, k), (i + 1, k)), 0)
            for f, value in enumerate(face(ul, ur, fl, fr, sl, sr)):
                fx[f, i, k] = value

    def update_plane(u_ref, q_ref, i, dst, j):
        change = [[fx[f, i, k] - fx[f, i - 1, k] for k in range(4)] for f in range(F)]
        for d, pairs in ((1, ((0, 2), (1, 3))), (2, ((0, 1), (2, 3)))):
            for even, odd in pairs:
                (ue, fe, se), (uo, fo, so) = sides(u_ref, q_ref, ((i, even), (i, odd)), d)
                inner = face(ue, uo, fe, fo, se, so)
                un, fn = [[turned(a, d - 1, -1) for a in part] for part in (ue, fe)]
                outer = face(uo, un, fo, fn, so, turned(se, d - 1, -1))
                for f in range(F):
                    change[f][even] = change[f][even] + (inner[f] - turned(outer[f], d - 1, 1))
                    change[f][odd] = change[f][odd] + (outer[f] - inner[f])
        for f in range(F):
            for k in range(4):
                dst[f, j, k] = u_ref[f, i, k] - HALF_STEP * change[f][k]

    loop(2, 4, lambda i: prim_plane(ext, q1, i), 2)
    loop(2, 3, lambda i: face_plane(ext, q1, i))
    pl.semaphore_wait(hello.at[0], 4)
    greet(hello.at[1], [4])
    loop(3, 2, lambda i: update_plane(ext, q1, i, mid, i), 2)

    def row_total(buffer, count, s, r):
        return send(buffer.at[pl.ds(0, count)], buffer.at[pl.ds(0, count)], s, r, peer(0, 1))

    row_total(code_x, NX - 1, cx_s, cx_r).wait()
    packed = jnp.zeros((1, 128), jnp.float32)
    for sx in range(NX):
        moved = pltpu.roll(code_x[sx], lax.rem(128 + (sx - mx) * NZ, 128), 1)
        packed = jnp.where((lane >= sx * NZ) & (lane < (sx + 1) * NZ), moved, packed)
    bundle[...] = packed
    code_z[mz] = packed

    def side(low):
        p, e, u = (jnp.where(low, 0, 6), jnp.where(low, 0, 5), jnp.where(low, 1, 5))
        loop(p, 2, lambda i: prim_plane(ext, q1, i), 2)
        loop(e, 2, lambda i: face_plane(ext, q1, i), 2)
        loop(u, 2, lambda i: update_plane(ext, q1, i, mid, i), 2)

    def ghost_planes(end, near, far):
        for c in ghost_loads(end):
            c.wait()

        def lines(t):
            return [
                jnp.concatenate([graw[t, f, h, pl.ds(py, 8, stride=2), :] for h in (0, 1)], axis=1)
                for f in range(F)
                for py in (0, 1)
            ]

        def put_start(f, k, value):
            ext[f, near, k] = value
            ext[f, far, k] = value

        def put_middle(f, k, value):
            gbuf[f, k] = 0.5 * ext[f, near, k] + 0.5 * value

        split_plane(lines(0), put_start)
        split_plane(lines(1), put_middle)

    def wait_low():
        @pl.when(jnp.logical_not(at_low))
        def _():
            halo_down().wait_send()
            halo_up().wait_recv()

        @pl.when(at_low)
        def _():
            ghost_planes(0, 1, 0)

    def wait_high():
        @pl.when(jnp.logical_not(at_high))
        def _():
            halo_up().wait_send()
            halo_down().wait_recv()

        @pl.when(at_high)
        def _():
            ghost_planes(1, 6, 7)

    odd = lax.rem(box, 2) == 1
    even = jnp.logical_not(odd)

    @pl.when(odd)
    def _():
        wait_low()

    @pl.when(even)
    def _():
        wait_high()

    side(odd)

    def second(prim, faces, update):
        loop(prim[0], prim[1], lambda i: prim_plane(mid, q2, i), 2)
        loop(faces[0], faces[1], lambda i: face_plane(mid, q2, i))
        loop(update, 2, lambda i: update_plane(mid, q2, i, fnew, i - 2), 2)

    first = jnp.where(odd, 1, 3)
    second((first, 4), (first, 3), first + 1)

    @pl.when(odd)
    def _():
        wait_high()

    @pl.when(even)
    def _():
        wait_low()

    side(even)

    scale = jnp.where(at_low, -0.0075 * 0.5, 0.0075 * 0.5)
    edge = jnp.where(at_low, 1, 5)
    for f in range(F):
        for k in range(4):
            face_sum[f, k] = fx[f, edge, k]

    for at_end, plane in ((at_low, 1), (at_high, 6)):

        @pl.when(at_end)
        def _():
            for f in range(F):
                mid[f, plane] = gbuf[f]

    pl.semaphore_wait(hello.at[1], 2)
    for dx in range(1, NX):
        signal(hello.at[2], grp=peer(dx, 0))
    steps = [8, 7, 9, 6, 10, 5, 11, 4, 12, 3, 13, 2, 14, 1, 15]
    for dz in steps:
        send(bundle, code_z.at[mz], cz_s, cz_r, peer(0, dz)).start()

    second((jnp.where(odd, 5, 1), 2), (jnp.where(odd, 4, 1), 2), jnp.where(odd, 4, 2))

    for f in range(F):
        for r in range(3):
            if r < 2:
                parts = [fnew[f, 2 * r + x, k] for x in (0, 1) for k in range(4)]
                factor = 0.125
            else:
                parts = [face_sum[f, k] + fx[f, edge, k] for k in range(4)]
                factor = scale
            while len(parts) > 1:
                parts = [a + b for a, b in zip(parts[::2], parts[1::2])]
            rec[pl.ds(8 * r, 8), f, :] = factor * parts[0]
    rec[REC] = jnp.zeros((F, CZ), jnp.float32)

    to_inv.wait()

    def fill(s, carry):
        slots[s] = rec[jnp.clip(inv_s[0, s], 0, REC)]
        return carry

    lax.fori_loop(0, NX * NZ, fill, 0, unroll=8)

    pl.semaphore_wait(hello.at[2], NX - 1)
    for dz in steps + [0]:
        for dx in (2, 1, 3, 0):
            if (dx, dz) != (0, 0):
                to = peer(dx, dz)
                send(slots.at[to], recv.at[me], rec_s, rec_r, to).start()
    recv[me] = slots[me]
    recv[NX * NZ] = jnp.zeros((F, CZ), jnp.float32)

    to_whole = jnp.where(col == cell(row), 1.0, 0.0).astype(jnp.bfloat16)

    def whole_plane(i):
        lines = [
            jnp.concatenate([fnew[f, i, 2 * py + pz] for pz in (0, 1)], axis=1)
            for f in range(F)
            for py in (0, 1)
        ]
        moved = exact_dot(jnp.concatenate(lines, axis=0), to_whole)
        for f in range(F):
            for py in (0, 1):
                at = 8 * (2 * f + py)
                for h in (0, 1):
                    part = moved[at : at + 8, 128 * h : 128 * (h + 1)]
                    fine_out[f, i, h, pl.ds(py, 8, stride=2), :] = part

    loop(0, 4, whole_plane)

    row_total(code_z, NZ - 1, cz_s, cz_r).wait()
    owner_z = lax.bitwise_and(lane, NZ - 1) == mz
    valid = owner_z & (lane < NX * NZ)
    source = lax.bitwise_and(lane, -NZ) + 1
    hits = [jnp.zeros((1, 128), jnp.int32) for _ in range(REC)]
    for sz in range(NZ):
        codes = jnp.where(valid, code_z[sz].astype(jnp.int32), 0)
        slot = source + sz
        for c in range(REC):
            average, is_face = codes == c + 1, codes == c + 33
            hits[c] = hits[c] + jnp.where(average, slot, jnp.where(is_face, slot + 128, 0))
    total = jnp.sum(
        jnp.concatenate(hits, axis=0).astype(jnp.float32), axis=1, keepdims=True
    ).astype(jnp.int32)
    total = jnp.broadcast_to(total, (REC, 128))
    of_face = total > 128
    found[...] = jnp.where(total == 0, NX * NZ, jnp.where(of_face, total - 129, total - 1))
    to_src = local(found, src_s, 10)
    to_src.start()
    load_state.wait()
    load_term.wait()
    for f in range(F):
        base = state_v[f]
        state_v[f] = jnp.where(
            total == 0, base, jnp.where(of_face, base - term_v[f], jnp.zeros_like(base))
        )
    to_src.wait()

    row_total(recv, NX * NZ - 1, rec_s, rec_r).wait()
    for c in range(REC):
        value = recv[jnp.clip(src_s[c, 0], 0, NX * NZ)]
        gathered[pl.ds(c, F, stride=REC), :] = value
    for f in range(F):
        coarse_out[f] = state_v[f] + gathered[pl.ds(REC * f, REC), :]


def store_kernel(fine_v, coarse_v, fine_out, coarse_out, sem):
    copies = [pltpu.make_async_copy(coarse_v, coarse_out, sem.at[2])]
    for h in (0, 1):
        part = fine_out.at[0, :, :, :, pl.ds(128 * h, 128)]
        copies.append(pltpu.make_async_copy(fine_v.at[:, :, h], part, sem.at[h]))
    for c in copies:
        c.start()
    for c in copies:
        c.wait()


def on_device(fine_state, patch_ghosts, coarse_state, coarse_face_term, dest_grp, dest_column):
    any_spec = pl.BlockSpec(memory_space=pl.ANY)
    vmem_spec = pl.BlockSpec(memory_space=pltpu.VMEM)
    vm, sm, f32, i32 = pltpu.VMEM, pltpu.SMEM, jnp.float32, jnp.int32
    dma = pltpu.SemaphoreType.DMA
    fine_new, coarse_new = pl.pallas_call(
        kernel,
        out_shape=(vm((F, 4, 2, 16, 128), f32), vm((F, REC, CZ), f32)),
        in_specs=[any_spec] * 6,
        out_specs=(vmem_spec, vmem_spec),
        scratch_shapes=[
            vm((F, 4, 2, 16, 128), f32),
            vm((2, F, 2, 16, 128), f32),
            vm((F, 8, 4, 8, 128), f32),
            vm((F, 8, 4, 8, 128), f32),
            vm((F, 8, 4, 8, 128), f32),
            vm((F, 8, 4, 8, 128), f32),
            vm((F, 8, 4, 8, 128), f32),
            vm((F, 4, 4, 8, 128), f32),
            vm((F, 4, 8, 128), f32),
            vm((F, 4, 8, 128), f32),
            vm((REC + 1, F, CZ), f32),
            vm((NX * NZ, F, CZ), f32),
            vm((NX * NZ + 1, F, CZ), f32),
            vm((F * REC, CZ), f32),
            vm((1, 128), f32),
            vm((NX, 1, 128), f32),
            vm((1, 128), f32),
            vm((NZ, 1, 128), f32),
            vm((1, 128), i32),
            vm((REC, 128), i32),
            vm((F, REC, CZ), f32),
            vm((F, REC, CZ), f32),
            sm((1, 1, REC), i32),
            sm((1, 1, REC), i32),
            sm((1, 128), i32),
            sm((REC, 128), i32),
            dma((11,)),
            dma((2,)),
            dma((2,)),
            dma,
            dma,
            dma,
            dma,
            dma,
            dma,
            pltpu.SemaphoreType.REGULAR((3,)),
        ],
        compiler_params=pltpu.CompilerParams(collective_id=0, has_side_effects=True),
    )(
        fine_state,
        patch_ghosts,
        coarse_state[0, 0].transpose(1, 0, 2),
        coarse_face_term[0, 0].transpose(1, 0, 2),
        dest_grp,
        dest_column,
    )
    fine_new, coarse_new = pl.pallas_call(
        store_kernel,
        out_shape=(
            jax.ShapeDtypeStruct(fine_state.shape, f32),
            jax.ShapeDtypeStruct((F, REC, CZ), f32),
        ),
        in_specs=[vmem_spec] * 2,
        out_specs=(any_spec, any_spec),
        scratch_shapes=[dma((3,))],
    )(
        pltpu.with_memory_space_constraint(fine_new, vm),
        pltpu.with_memory_space_constraint(coarse_new, vm),
    )
    return fine_new, coarse_new.transpose(1, 0, 2)[None, None]


def solution(mesh):
    in_specs = (
        P("grp", None, "box", None, None),
        P("grp", None, None, None, None, None),
        P("grp", "box", None, None, None),
        P("grp", "box", None, None, None),
        P("grp", "box", None),
        P("grp", "box", None),
    )
    out_specs = (P("grp", None, "box", None, None), P("grp", "box", None, None, None))
    return jax.shard_map(
        on_device, mesh=mesh, in_specs=in_specs, out_specs=out_specs, check_vma=False
    )
```

```python
import jax
import jax.numpy as jnp
from jax import lax
from jax.experimental import pallas as pl
from jax.experimental.pallas import tpu as pltpu
from jax.sharding import PartitionSpec as P

MESH = pl.DeviceIdType.MESH
HALF_STEP = 0.03
NX, NZ, NB = 4, 16, 8
F, REC, NAVG, CZ = 5, 24, 16, 128


def primitives(u):
    inverse = 1.0 / u[0]
    v = [u[1] * inverse, u[2] * inverse, u[3] * inverse]
    kinetic = 0.5 * (u[1] * v[0] + u[2] * v[1] + u[3] * v[2])
    pressure = 0.4 * (u[4] - kinetic)
    sound = jnp.sqrt(1.4 * pressure * inverse)
    return v + [pressure, sound]


def flux(u, q, d):
    out = [u[1 + d]]
    for m in range(3):
        f = u[1 + m] * q[d]
        out.append(f + q[3] if m == d else f)
    out.append((u[4] + q[3]) * q[d])
    return out


def face(ul, ur, fl, fr, sl, sr):
    biggest = jnp.maximum(sl, sr)
    return [(fl[f] + fr[f]) - biggest * (ur[f] - ul[f]) for f in range(F)]


def exact_dot(x, to):
    total = None
    for _ in range(3):
        part = x.astype(jnp.bfloat16)
        x = x - part.astype(jnp.float32)
        moved = jnp.dot(part, to, preferred_element_type=jnp.float32)
        total = moved if total is None else total + moved
    return total


def turned(a, axis, shift):
    return pltpu.roll(a, shift % (8, 128)[axis], axis)


def kernel(
    fine, ghosts, state, term, dgrp, dcol,
    fine_out, coarse_out,
    raw, graw, ext, mid, q1, q2, fx, fnew, gbuf, face_sum, rec, slots, recv, gathered,
    code_tx, code_x, bundle, code_z, table, found, state_v, term_v,
    dg_s, dc_s, inv_s, src_s,
    in_sem, halo_s, halo_r, cx_s, cx_r, cz_s, cz_r, rec_s, rec_r, hello,
):
    me = lax.axis_index("grp")
    box = lax.axis_index("box")
    at_low = box == 0
    at_high = box == NB - 1
    mx, mz = lax.div(me, NZ), lax.rem(me, NZ)

    def peer(dx, dz):
        return lax.rem(mx + dx, NX) * NZ + lax.rem(mz + dz, NZ)

    def signal(sem, **where):
        pl.semaphore_signal(sem, inc=1, device_id=where, device_id_type=MESH)

    def greet(sem, steps):
        for dz in steps:
            signal(sem, grp=peer(0, dz))
            signal(sem, grp=peer(0, NZ - dz))

    barrier = pltpu.get_barrier_semaphore()

    @pl.when(jnp.logical_not(at_low))
    def _():
        signal(barrier, box=box - 1)

    @pl.when(jnp.logical_not(at_high))
    def _():
        signal(barrier, box=box + 1)

    greet(barrier, [1, 2])
    for dx in range(1, NX):
        signal(barrier, grp=peer(dx, 0))

    def local(src, dst, at):
        return pltpu.make_async_copy(src, dst, in_sem.at[at])

    def halves(src, dst, at):
        return [
            local(src.at[:, :, pl.ds(128 * h, 128)], dst.at[:, h], at + h) for h in (0, 1)
        ]

    load_fine = [
        local(fine.at[0, :, :, :, pl.ds(128 * h, 128)], raw.at[:, :, h], h) for h in (0, 1)
    ]
    load_dg = local(dgrp, dg_s, 2)
    load_dc = local(dcol, dc_s, 3)
    load_state = local(state, state_v, 4)
    load_term = local(term, term_v, 5)
    for c in load_fine:
        c.start()
    load_dg.start()
    load_dc.start()

    def ghost_loads(end):
        return [c for t in (0, 1) for c in halves(ghosts.at[0, t, end], graw.at[t], 6 + 2 * t)]

    @pl.when(at_low)
    def _():
        for c in ghost_loads(0):
            c.start()

    @pl.when(at_high)
    def _():
        for c in ghost_loads(1):
            c.start()

    load_state.start()
    load_term.start()

    lane = lax.broadcasted_iota(jnp.int32, (1, 128), 1)
    load_dg.wait()
    load_dc.wait()
    live_face = jnp.where(at_low | at_high, 1, 0)
    which = jnp.full((1, 128), REC, jnp.int32)
    code = jnp.zeros((1, 128), jnp.int32)
    for r in range(REC):
        hit = lane == dg_s[0, 0, r]
        which = jnp.where(hit, r, which)
        value = dc_s[0, 0, r] + 1
        if r >= NAVG:
            value = (value + 32) * live_face
        code = jnp.where(hit, value, code)
    code_tx[...] = code.astype(jnp.float32)
    table[...] = which
    to_inv = local(table, inv_s, 10)
    to_inv.start()

    row = lax.broadcasted_iota(jnp.int32, (256, 256), 0)
    col = lax.broadcasted_iota(jnp.int32, (256, 256), 1)

    def cell(split):
        return 2 * lax.bitwise_and(split, 127) + lax.shift_right_logical(split, 7)

    to_split = jnp.where(row == cell(col), 1.0, 0.0).astype(jnp.bfloat16)

    def split_plane(lines, put):
        moved = exact_dot(jnp.concatenate(lines, axis=0), to_split)
        for f in range(F):
            for py in (0, 1):
                at = 8 * (2 * f + py)
                for pz in (0, 1):
                    put(f, 2 * py + pz, moved[at : at + 8, 128 * pz : 128 * (pz + 1)])

    def loop(start, count, body, unroll=1):
        def step(i, carry):
            body(start + i)
            return carry

        lax.fori_loop(0, count, step, 0, unroll=unroll)

    for c in load_fine:
        c.wait()

    def split_fine(i):
        lines = [
            jnp.concatenate([raw[f, i, h, pl.ds(py, 8, stride=2), :] for h in (0, 1)], axis=1)
            for f in range(F)
            for py in (0, 1)
        ]

        def put(f, k, value):
            ext[f, i + 2, k] = value

        split_plane(lines, put)

    loop(0, 4, split_fine, 4)

    pl.semaphore_wait(barrier, NX + 3 + jnp.where(at_low | at_high, 1, 2))

    def halo_down():
        return pltpu.make_async_remote_copy(
            ext.at[:, pl.ds(2, 2)], ext.at[:, pl.ds(6, 2)], halo_s.at[0], halo_r.at[0],
            device_id={"box": box - 1}, device_id_type=MESH,
        )

    def halo_up():
        return pltpu.make_async_remote_copy(
            ext.at[:, pl.ds(4, 2)], ext.at[:, pl.ds(0, 2)], halo_s.at[1], halo_r.at[1],
            device_id={"box": box + 1}, device_id_type=MESH,
        )

    odd = lax.rem(box, 2) == 1
    even = jnp.logical_not(odd)

    @pl.when(even)
    def _():
        halo_up().start()

    @pl.when(jnp.logical_not(at_low))
    def _():
        halo_down().start()

    @pl.when(odd & jnp.logical_not(at_high))
    def _():
        halo_up().start()

    greet(hello.at[0], [1, 2])

    def send(src, dst, s, r, to):
        return pltpu.make_async_remote_copy(
            src, dst, s, r, device_id={"grp": to}, device_id_type=MESH
        )

    for dx in range(1, NX):
        send(code_tx, code_x.at[mx], cx_s, cx_r, peer(dx, 0)).start()
    code_x[mx] = code_tx[...]

    def prim_plane(u_ref, q_ref, i):
        for k in range(4):
            q = primitives([u_ref[f, i, k] for f in range(F)])
            for f in range(F):
                q_ref[f, i, k] = q[f]

    def sides(u_ref, q_ref, places, d):
        out = []
        for i, k in places:
            u, q = [[ref[f, i, k] for f in range(F)] for ref in (u_ref, q_ref)]
            out.append((u, flux(u, q, d), jnp.abs(q[d]) + q[4]))
        return out

    def face_plane(u_ref, q_ref, i):
        for k in range(4):
            (ul, fl, sl), (ur, fr, sr) = sides(u_ref, q_ref, ((i, k), (i + 1, k)), 0)
            for f, value in enumerate(face(ul, ur, fl, fr, sl, sr)):
                fx[f, i, k] = value

    def update_plane(u_ref, q_ref, i, dst, j):
        change = [[fx[f, i, k] - fx[f, i - 1, k] for k in range(4)] for f in range(F)]
        for d, pairs in ((1, ((0, 2), (1, 3))), (2, ((0, 1), (2, 3)))):
            for even, odd in pairs:
                (ue, fe, se), (uo, fo, so) = sides(u_ref, q_ref, ((i, even), (i, odd)), d)
                inner = face(ue, uo, fe, fo, se, so)
                un, fn = [[turned(a, d - 1, -1) for a in part] for part in (ue, fe)]
                outer = face(uo, un, fo, fn, so, turned(se, d - 1, -1))
                for f in range(F):
                    change[f][even] = change[f][even] + (inner[f] - turned(outer[f], d - 1, 1))
                    change[f][odd] = change[f][odd] + (outer[f] - inner[f])
        for f in range(F):
            for k in range(4):
                dst[f, j, k] = u_ref[f, i, k] - HALF_STEP * change[f][k]

    loop(2, 4, lambda i: prim_plane(ext, q1, i), 2)
    loop(2, 3, lambda i: face_plane(ext, q1, i))
    pl.semaphore_wait(hello.at[0], 4)
    greet(hello.at[1], [4])
    loop(3, 2, lambda i: update_plane(ext, q1, i, mid, i), 2)

    def row_total(buffer, count, s, r):
        return send(buffer.at[pl.ds(0, count)], buffer.at[pl.ds(0, count)], s, r, peer(0, 1))

    row_total(code_x, NX - 1, cx_s, cx_r).wait()
    packed = jnp.zeros((1, 128), jnp.float32)
    for sx in range(NX):
        moved = pltpu.roll(code_x[sx], lax.rem(128 + (sx - mx) * NZ, 128), 1)
        packed = jnp.where((lane >= sx * NZ) & (lane < (sx + 1) * NZ), moved, packed)
    bundle[...] = packed
    code_z[mz] = packed

    def side(low):
        p, e, u = (jnp.where(low, 0, 6), jnp.where(low, 0, 5), jnp.where(low, 1, 5))
        loop(p, 2, lambda i: prim_plane(ext, q1, i), 2)
        loop(e, 2, lambda i: face_plane(ext, q1, i), 2)
        loop(u, 2, lambda i: update_plane(ext, q1, i, mid, i), 2)

    def ghost_planes(end, near, far):
        for c in ghost_loads(end):
            c.wait()

        def lines(t):
            return [
                jnp.concatenate([graw[t, f, h, pl.ds(py, 8, stride=2), :] for h in (0, 1)], axis=1)
                for f in range(F)
                for py in (0, 1)
            ]

        def put_start(f, k, value):
            ext[f, near, k] = value
            ext[f, far, k] = value

        def put_middle(f, k, value):
            gbuf[f, k] = 0.5 * ext[f, near, k] + 0.5 * value

        split_plane(lines(0), put_start)
        split_plane(lines(1), put_middle)

    def wait_low():
        @pl.when(jnp.logical_not(at_low))
        def _():
            halo_down().wait_send()
            halo_up().wait_recv()

        @pl.when(at_low)
        def _():
            ghost_planes(0, 1, 0)

    def wait_high():
        @pl.when(jnp.logical_not(at_high))
        def _():
            halo_up().wait_send()
            halo_down().wait_recv()

        @pl.when(at_high)
        def _():
            ghost_planes(1, 6, 7)

    @pl.when(odd)
    def _():
        wait_low()

    @pl.when(even)
    def _():
        wait_high()

    side(odd)

    def second(prim, faces, update):
        loop(prim[0], prim[1], lambda i: prim_plane(mid, q2, i), 2)
        loop(faces[0], faces[1], lambda i: face_plane(mid, q2, i))
        loop(update, 2, lambda i: update_plane(mid, q2, i, fnew, i - 2), 2)

    first = jnp.where(odd, 1, 3)
    second((first, 4), (first, 3), first + 1)

    @pl.when(odd)
    def _():
        wait_high()

    @pl.when(even)
    def _():
        wait_low()

    side(even)

    scale = jnp.where(at_low, -0.0075 * 0.5, 0.0075 * 0.5)
    edge = jnp.where(at_low, 1, 5)
    for f in range(F):
        for k in range(4):
            face_sum[f, k] = fx[f, edge, k]

    for at_end, plane in ((at_low, 1), (at_high, 6)):

        @pl.when(at_end)
        def _():
            for f in range(F):
                mid[f, plane] = gbuf[f]

    pl.semaphore_wait(hello.at[1], 2)
    for dx in range(1, NX):
        signal(hello.at[2], grp=peer(dx, 0))
    steps = [8, 7, 9, 6, 10, 5, 11, 4, 12, 3, 13, 2, 14, 1, 15]

    second((jnp.where(odd, 5, 1), 2), (jnp.where(odd, 4, 1), 2), jnp.where(odd, 4, 2))

    for f in range(F):
        for r in range(3):
            if r < 2:
                parts = [fnew[f, 2 * r + x, k] for x in (0, 1) for k in range(4)]
                factor = 0.125
            else:
                parts = [face_sum[f, k] + fx[f, edge, k] for k in range(4)]
                factor = scale
            while len(parts) > 1:
                parts = [a + b for a, b in zip(parts[::2], parts[1::2])]
            rec[pl.ds(8 * r, 8), f, :] = factor * parts[0]
    rec[REC] = jnp.zeros((F, CZ), jnp.float32)

    to_inv.wait()

    def fill(s, carry):
        slots[s] = rec[jnp.clip(inv_s[0, s], 0, REC)]
        return carry

    lax.fori_loop(0, NX * NZ, fill, 0, unroll=8)

    pl.semaphore_wait(hello.at[2], NX - 1)
    for dz in steps + [0]:
        if dz == 6:
            for to_z in steps:
                send(bundle, code_z.at[mz], cz_s, cz_r, peer(0, to_z)).start()
        for dx in (2, 1, 3, 0):
            if (dx, dz) != (0, 0):
                to = peer(dx, dz)
                send(slots.at[to], recv.at[me], rec_s, rec_r, to).start()
    recv[me] = slots[me]
    recv[NX * NZ] = jnp.zeros((F, CZ), jnp.float32)

    to_whole = jnp.where(col == cell(row), 1.0, 0.0).astype(jnp.bfloat16)

    def whole_plane(i):
        lines = [
            jnp.concatenate([fnew[f, i, 2 * py + pz] for pz in (0, 1)], axis=1)
            for f in range(F)
            for py in (0, 1)
        ]
        moved = exact_dot(jnp.concatenate(lines, axis=0), to_whole)
        for f in range(F):
            for py in (0, 1):
                at = 8 * (2 * f + py)
                for h in (0, 1):
                    part = moved[at : at + 8, 128 * h : 128 * (h + 1)]
                    fine_out[f, i, h, pl.ds(py, 8, stride=2), :] = part

    loop(0, 4, whole_plane)

    row_total(code_z, NZ - 1, cz_s, cz_r).wait()
    owner_z = lax.bitwise_and(lane, NZ - 1) == mz
    valid = owner_z & (lane < NX * NZ)
    source = lax.bitwise_and(lane, -NZ) + 1
    hits = [jnp.zeros((1, 128), jnp.int32) for _ in range(REC)]
    for sz in range(NZ):
        codes = jnp.where(valid, code_z[sz].astype(jnp.int32), 0)
        slot = source + sz
        for c in range(REC):
            average, is_face = codes == c + 1, codes == c + 33
            hits[c] = hits[c] + jnp.where(average, slot, jnp.where(is_face, slot + 128, 0))
    total = jnp.sum(
        jnp.concatenate(hits, axis=0).astype(jnp.float32), axis=1, keepdims=True
    ).astype(jnp.int32)
    total = jnp.broadcast_to(total, (REC, 128))
    of_face = total > 128
    found[...] = jnp.where(total == 0, NX * NZ, jnp.where(of_face, total - 129, total - 1))
    to_src = local(found, src_s, 10)
    to_src.start()
    load_state.wait()
    load_term.wait()
    for f in range(F):
        base = state_v[f]
        state_v[f] = jnp.where(
            total == 0, base, jnp.where(of_face, base - term_v[f], jnp.zeros_like(base))
        )
    to_src.wait()

    row_total(recv, NX * NZ - 1, rec_s, rec_r).wait()
    for c in range(REC):
        value = recv[jnp.clip(src_s[c, 0], 0, NX * NZ)]
        gathered[pl.ds(c, F, stride=REC), :] = value
    for f in range(F):
        coarse_out[f] = state_v[f] + gathered[pl.ds(REC * f, REC), :]


def store_kernel(fine_v, coarse_v, fine_out, coarse_out, sem):
    copies = [pltpu.make_async_copy(coarse_v, coarse_out, sem.at[2])]
    for h in (0, 1):
        part = fine_out.at[0, :, :, :, pl.ds(128 * h, 128)]
        copies.append(pltpu.make_async_copy(fine_v.at[:, :, h], part, sem.at[h]))
    for c in copies:
        c.start()
    for c in copies:
        c.wait()


def on_device(fine_state, patch_ghosts, coarse_state, coarse_face_term, dest_grp, dest_column):
    any_spec = pl.BlockSpec(memory_space=pl.ANY)
    vmem_spec = pl.BlockSpec(memory_space=pltpu.VMEM)
    vm, sm, f32, i32 = pltpu.VMEM, pltpu.SMEM, jnp.float32, jnp.int32
    dma = pltpu.SemaphoreType.DMA
    fine_new, coarse_new = pl.pallas_call(
        kernel,
        out_shape=(vm((F, 4, 2, 16, 128), f32), vm((F, REC, CZ), f32)),
        in_specs=[any_spec] * 6,
        out_specs=(vmem_spec, vmem_spec),
        scratch_shapes=[
            vm((F, 4, 2, 16, 128), f32),
            vm((2, F, 2, 16, 128), f32),
            vm((F, 8, 4, 8, 128), f32),
            vm((F, 8, 4, 8, 128), f32),
            vm((F, 8, 4, 8, 128), f32),
            vm((F, 8, 4, 8, 128), f32),
            vm((F, 8, 4, 8, 128), f32),
            vm((F, 4, 4, 8, 128), f32),
            vm((F, 4, 8, 128), f32),
            vm((F, 4, 8, 128), f32),
            vm((REC + 1, F, CZ), f32),
            vm((NX * NZ, F, CZ), f32),
            vm((NX * NZ + 1, F, CZ), f32),
            vm((F * REC, CZ), f32),
            vm((1, 128), f32),
            vm((NX, 1, 128), f32),
            vm((1, 128), f32),
            vm((NZ, 1, 128), f32),
            vm((1, 128), i32),
            vm((REC, 128), i32),
            vm((F, REC, CZ), f32),
            vm((F, REC, CZ), f32),
            sm((1, 1, REC), i32),
            sm((1, 1, REC), i32),
            sm((1, 128), i32),
            sm((REC, 128), i32),
            dma((11,)),
            dma((2,)),
            dma((2,)),
            dma,
            dma,
            dma,
            dma,
            dma,
            dma,
            pltpu.SemaphoreType.REGULAR((3,)),
        ],
        compiler_params=pltpu.CompilerParams(collective_id=0, has_side_effects=True),
    )(
        fine_state,
        patch_ghosts,
        coarse_state[0, 0].transpose(1, 0, 2),
        coarse_face_term[0, 0].transpose(1, 0, 2),
        dest_grp,
        dest_column,
    )
    fine_new, coarse_new = pl.pallas_call(
        store_kernel,
        out_shape=(
            jax.ShapeDtypeStruct(fine_state.shape, f32),
            jax.ShapeDtypeStruct((F, REC, CZ), f32),
        ),
        in_specs=[vmem_spec] * 2,
        out_specs=(any_spec, any_spec),
        scratch_shapes=[dma((3,))],
    )(
        pltpu.with_memory_space_constraint(fine_new, vm),
        pltpu.with_memory_space_constraint(coarse_new, vm),
    )
    return fine_new, coarse_new.transpose(1, 0, 2)[None, None]


def solution(mesh):
    in_specs = (
        P("grp", None, "box", None, None),
        P("grp", None, None, None, None, None),
        P("grp", "box", None, None, None),
        P("grp", "box", None, None, None),
        P("grp", "box", None),
        P("grp", "box", None),
    )
    out_specs = (P("grp", None, "box", None, None), P("grp", "box", None, None, None))
    return jax.shard_map(
        on_device, mesh=mesh, in_specs=in_specs, out_specs=out_specs, check_vma=False
    )
```

```python
import jax
import jax.numpy as jnp
from jax import lax
from jax.experimental import pallas as pl
from jax.experimental.pallas import tpu as pltpu
from jax.sharding import PartitionSpec as P

MESH = pl.DeviceIdType.MESH
HALF_STEP = 0.03
NX, NZ, NB = 4, 16, 8
F, REC, NAVG, CZ = 5, 24, 16, 128


def primitives(u):
    inverse = 1.0 / u[0]
    v = [u[1] * inverse, u[2] * inverse, u[3] * inverse]
    kinetic = 0.5 * (u[1] * v[0] + u[2] * v[1] + u[3] * v[2])
    pressure = 0.4 * (u[4] - kinetic)
    sound = jnp.sqrt(1.4 * pressure * inverse)
    return v + [pressure, sound]


def flux(u, q, d):
    out = [u[1 + d]]
    for m in range(3):
        f = u[1 + m] * q[d]
        out.append(f + q[3] if m == d else f)
    out.append((u[4] + q[3]) * q[d])
    return out


def face(ul, ur, fl, fr, sl, sr):
    biggest = jnp.maximum(sl, sr)
    return [(fl[f] + fr[f]) - biggest * (ur[f] - ul[f]) for f in range(F)]


def exact_dot(x, to):
    total = None
    for _ in range(3):
        part = x.astype(jnp.bfloat16)
        x = x - part.astype(jnp.float32)
        moved = jnp.dot(part, to, preferred_element_type=jnp.float32)
        total = moved if total is None else total + moved
    return total


def turned(a, axis, shift):
    return pltpu.roll(a, shift % (8, 128)[axis], axis)


def kernel(
    fine, ghosts, state, term, dgrp, dcol,
    fine_out, coarse_out,
    raw, graw, ext, mid, q1, q2, fx, fnew, gbuf, face_sum, rec, slots, recv, gathered,
    code_tx, code_x, bundle, code_z, table, found, state_v, term_v,
    dg_s, dc_s, inv_s, src_s,
    in_sem, halo_s, halo_r, cx_s, cx_r, cz_s, cz_r, rec_s, rec_r, hello,
):
    me = lax.axis_index("grp")
    box = lax.axis_index("box")
    at_low = box == 0
    at_high = box == NB - 1
    mx, mz = lax.div(me, NZ), lax.rem(me, NZ)

    def peer(dx, dz):
        return lax.rem(mx + dx, NX) * NZ + lax.rem(mz + dz, NZ)

    def signal(sem, **where):
        pl.semaphore_signal(sem, inc=1, device_id=where, device_id_type=MESH)

    def greet(sem, steps):
        for dz in steps:
            signal(sem, grp=peer(0, dz))
            signal(sem, grp=peer(0, NZ - dz))

    barrier = pltpu.get_barrier_semaphore()

    @pl.when(jnp.logical_not(at_low))
    def _():
        signal(barrier, box=box - 1)

    @pl.when(jnp.logical_not(at_high))
    def _():
        signal(barrier, box=box + 1)

    greet(barrier, [1, 2])
    for dx in range(1, NX):
        signal(barrier, grp=peer(dx, 0))

    def local(src, dst, at):
        return pltpu.make_async_copy(src, dst, in_sem.at[at])

    def halves(src, dst, at):
        return [
            local(src.at[:, :, pl.ds(128 * h, 128)], dst.at[:, h], at + h) for h in (0, 1)
        ]

    load_fine = [
        local(fine.at[0, :, :, :, pl.ds(128 * h, 128)], raw.at[:, :, h], h) for h in (0, 1)
    ]
    load_dg = local(dgrp, dg_s, 2)
    load_dc = local(dcol, dc_s, 3)
    load_state = local(state, state_v, 4)
    load_term = local(term, term_v, 5)
    for c in load_fine:
        c.start()
    load_dg.start()
    load_dc.start()

    def ghost_loads(end):
        return [c for t in (0, 1) for c in halves(ghosts.at[0, t, end], graw.at[t], 6 + 2 * t)]

    @pl.when(at_low)
    def _():
        for c in ghost_loads(0):
            c.start()

    @pl.when(at_high)
    def _():
        for c in ghost_loads(1):
            c.start()

    load_state.start()
    load_term.start()

    lane = lax.broadcasted_iota(jnp.int32, (1, 128), 1)
    load_dg.wait()
    load_dc.wait()
    live_face = jnp.where(at_low | at_high, 1, 0)
    which = jnp.full((1, 128), REC, jnp.int32)
    code = jnp.zeros((1, 128), jnp.int32)
    for r in range(REC):
        hit = lane == dg_s[0, 0, r]
        which = jnp.where(hit, r, which)
        value = dc_s[0, 0, r] + 1
        if r >= NAVG:
            value = (value + 32) * live_face
        code = jnp.where(hit, value, code)
    code_tx[...] = code.astype(jnp.float32)
    table[...] = which
    to_inv = local(table, inv_s, 10)
    to_inv.start()

    row = lax.broadcasted_iota(jnp.int32, (256, 256), 0)
    col = lax.broadcasted_iota(jnp.int32, (256, 256), 1)

    def cell(split):
        return 2 * lax.bitwise_and(split, 127) + lax.shift_right_logical(split, 7)

    to_split = jnp.where(row == cell(col), 1.0, 0.0).astype(jnp.bfloat16)

    def split_plane(lines, put):
        moved = exact_dot(jnp.concatenate(lines, axis=0), to_split)
        for f in range(F):
            for py in (0, 1):
                at = 8 * (2 * f + py)
                for pz in (0, 1):
                    put(f, 2 * py + pz, moved[at : at + 8, 128 * pz : 128 * (pz + 1)])

    def loop(start, count, body, unroll=1):
        def step(i, carry):
            body(start + i)
            return carry

        lax.fori_loop(0, count, step, 0, unroll=unroll)

    for c in load_fine:
        c.wait()

    def split_fine(i):
        lines = [
            jnp.concatenate([raw[f, i, h, pl.ds(py, 8, stride=2), :] for h in (0, 1)], axis=1)
            for f in range(F)
            for py in (0, 1)
        ]

        def put(f, k, value):
            ext[f, i + 2, k] = value

        split_plane(lines, put)

    loop(0, 4, split_fine, 4)

    pl.semaphore_wait(barrier, NX + 3 + jnp.where(at_low | at_high, 1, 2))

    def halo_down():
        return pltpu.make_async_remote_copy(
            ext.at[:, pl.ds(2, 2)], ext.at[:, pl.ds(6, 2)], halo_s.at[0], halo_r.at[0],
            device_id={"box": box - 1}, device_id_type=MESH,
        )

    def halo_up():
        return pltpu.make_async_remote_copy(
            ext.at[:, pl.ds(4, 2)], ext.at[:, pl.ds(0, 2)], halo_s.at[1], halo_r.at[1],
            device_id={"box": box + 1}, device_id_type=MESH,
        )

    odd = lax.rem(box, 2) == 1
    even = jnp.logical_not(odd)

    @pl.when(even)
    def _():
        halo_up().start()

    @pl.when(jnp.logical_not(at_low))
    def _():
        halo_down().start()

    @pl.when(odd & jnp.logical_not(at_high))
    def _():
        halo_up().start()

    greet(hello.at[0], [1, 2])

    def send(src, dst, s, r, to):
        return pltpu.make_async_remote_copy(
            src, dst, s, r, device_id={"grp": to}, device_id_type=MESH
        )

    for dx in range(1, NX):
        send(code_tx, code_x.at[mx], cx_s, cx_r, peer(dx, 0)).start()
    code_x[mx] = code_tx[...]

    def prim_plane(u_ref, q_ref, i):
        for k in range(4):
            q = primitives([u_ref[f, i, k] for f in range(F)])
            for f in range(F):
                q_ref[f, i, k] = q[f]

    def sides(u_ref, q_ref, places, d):
        out = []
        for i, k in places:
            u, q = [[ref[f, i, k] for f in range(F)] for ref in (u_ref, q_ref)]
            out.append((u, flux(u, q, d), jnp.abs(q[d]) + q[4]))
        return out

    def face_plane(u_ref, q_ref, i):
        for k in range(4):
            (ul, fl, sl), (ur, fr, sr) = sides(u_ref, q_ref, ((i, k), (i + 1, k)), 0)
            for f, value in enumerate(face(ul, ur, fl, fr, sl, sr)):
                fx[f, i, k] = value

    def update_plane(u_ref, q_ref, i, dst, j):
        change = [[fx[f, i, k] - fx[f, i - 1, k] for k in range(4)] for f in range(F)]
        for d, pairs in ((1, ((0, 2), (1, 3))), (2, ((0, 1), (2, 3)))):
            for even, odd in pairs:
                (ue, fe, se), (uo, fo, so) = sides(u_ref, q_ref, ((i, even), (i, odd)), d)
                inner = face(ue, uo, fe, fo, se, so)
                un, fn = [[turned(a, d - 1, -1) for a in part] for part in (ue, fe)]
                outer = face(uo, un, fo, fn, so, turned(se, d - 1, -1))
                for f in range(F):
                    change[f][even] = change[f][even] + (inner[f] - turned(outer[f], d - 1, 1))
                    change[f][odd] = change[f][odd] + (outer[f] - inner[f])
        for f in range(F):
            for k in range(4):
                dst[f, j, k] = u_ref[f, i, k] - HALF_STEP * change[f][k]

    loop(2, 4, lambda i: prim_plane(ext, q1, i), 2)
    loop(2, 3, lambda i: face_plane(ext, q1, i))
    pl.semaphore_wait(hello.at[0], 4)
    greet(hello.at[1], [4])
    loop(3, 2, lambda i: update_plane(ext, q1, i, mid, i), 2)

    def row_total(buffer, count, s, r):
        return send(buffer.at[pl.ds(0, count)], buffer.at[pl.ds(0, count)], s, r, peer(0, 1))

    row_total(code_x, NX - 1, cx_s, cx_r).wait()
    packed = jnp.zeros((1, 128), jnp.float32)
    for sx in range(NX):
        moved = pltpu.roll(code_x[sx], lax.rem(128 + (sx - mx) * NZ, 128), 1)
        packed = jnp.where((lane >= sx * NZ) & (lane < (sx + 1) * NZ), moved, packed)
    bundle[...] = packed
    code_z[mz] = packed

    def side(low):
        p, e, u = (jnp.where(low, 0, 6), jnp.where(low, 0, 5), jnp.where(low, 1, 5))
        loop(p, 2, lambda i: prim_plane(ext, q1, i), 2)
        loop(e, 2, lambda i: face_plane(ext, q1, i), 2)
        loop(u, 2, lambda i: update_plane(ext, q1, i, mid, i), 2)

    def ghost_planes(end, near, far):
        for c in ghost_loads(end):
            c.wait()

        def lines(t):
            return [
                jnp.concatenate([graw[t, f, h, pl.ds(py, 8, stride=2), :] for h in (0, 1)], axis=1)
                for f in range(F)
                for py in (0, 1)
            ]

        def put_start(f, k, value):
            ext[f, near, k] = value
            ext[f, far, k] = value

        def put_middle(f, k, value):
            gbuf[f, k] = 0.5 * ext[f, near, k] + 0.5 * value

        split_plane(lines(0), put_start)
        split_plane(lines(1), put_middle)

    def wait_low():
        @pl.when(jnp.logical_not(at_low))
        def _():
            halo_down().wait_send()
            halo_up().wait_recv()

        @pl.when(at_low)
        def _():
            ghost_planes(0, 1, 0)

    def wait_high():
        @pl.when(jnp.logical_not(at_high))
        def _():
            halo_up().wait_send()
            halo_down().wait_recv()

        @pl.when(at_high)
        def _():
            ghost_planes(1, 6, 7)

    @pl.when(odd)
    def _():
        wait_low()

    @pl.when(even)
    def _():
        wait_high()

    side(odd)

    def second(prim, faces, update):
        loop(prim[0], prim[1], lambda i: prim_plane(mid, q2, i), 2)
        loop(faces[0], faces[1], lambda i: face_plane(mid, q2, i))
        loop(update, 2, lambda i: update_plane(mid, q2, i, fnew, i - 2), 2)

    first = jnp.where(odd, 1, 3)
    second((first, 4), (first, 3), first + 1)

    @pl.when(odd)
    def _():
        wait_high()

    @pl.when(even)
    def _():
        wait_low()

    side(even)

    scale = jnp.where(at_low, -0.0075 * 0.5, 0.0075 * 0.5)
    edge = jnp.where(at_low, 1, 5)
    for f in range(F):
        for k in range(4):
            face_sum[f, k] = fx[f, edge, k]

    for at_end, plane in ((at_low, 1), (at_high, 6)):

        @pl.when(at_end)
        def _():
            for f in range(F):
                mid[f, plane] = gbuf[f]

    pl.semaphore_wait(hello.at[1], 2)
    for dx in range(1, NX):
        signal(hello.at[2], grp=peer(dx, 0))
    steps = [8, 7, 9, 6, 10, 5, 11, 4, 12, 3, 13, 2, 14, 1, 15]
    for dz in steps:
        send(bundle, code_z.at[mz], cz_s, cz_r, peer(0, dz)).start()

    second((jnp.where(odd, 5, 1), 2), (jnp.where(odd, 4, 1), 2), jnp.where(odd, 4, 2))

    for f in range(F):
        for r in range(3):
            if r < 2:
                parts = [fnew[f, 2 * r + x, k] for x in (0, 1) for k in range(4)]
                factor = 0.125
            else:
                parts = [face_sum[f, k] + fx[f, edge, k] for k in range(4)]
                factor = scale
            while len(parts) > 1:
                parts = [a + b for a, b in zip(parts[::2], parts[1::2])]
            rec[pl.ds(8 * r, 8), f, :] = factor * parts[0]
    rec[REC] = jnp.zeros((F, CZ), jnp.float32)

    to_inv.wait()

    def fill(s, carry):
        slots[s] = rec[jnp.clip(inv_s[0, s], 0, REC)]
        return carry

    lax.fori_loop(0, NX * NZ, fill, 0, unroll=8)

    pl.semaphore_wait(hello.at[2], NX - 1)
    for dz in steps + [0]:
        for dx in (2, 1, 3, 0):
            if (dx, dz) != (0, 0):
                to = peer(dx, dz)
                send(slots.at[to], recv.at[me], rec_s, rec_r, to).start()
    recv[me] = slots[me]
    recv[NX * NZ] = jnp.zeros((F, CZ), jnp.float32)

    to_whole = jnp.where(col == cell(row), 1.0, 0.0).astype(jnp.bfloat16)

    def whole_plane(i):
        lines = [
            jnp.concatenate([fnew[f, i, 2 * py + pz] for pz in (0, 1)], axis=1)
            for f in range(F)
            for py in (0, 1)
        ]
        moved = exact_dot(jnp.concatenate(lines, axis=0), to_whole)
        for f in range(F):
            for py in (0, 1):
                at = 8 * (2 * f + py)
                for h in (0, 1):
                    part = moved[at : at + 8, 128 * h : 128 * (h + 1)]
                    fine_out[f, i, h, pl.ds(py, 8, stride=2), :] = part

    loop(0, 4, whole_plane)

    row_total(code_z, NZ - 1, cz_s, cz_r).wait()
    owner_z = lax.bitwise_and(lane, NZ - 1) == mz
    valid = owner_z & (lane < NX * NZ)
    source = lax.bitwise_and(lane, -NZ) + 1
    hits = [jnp.zeros((1, 128), jnp.int32) for _ in range(REC)]
    for sz in range(NZ):
        codes = jnp.where(valid, code_z[sz].astype(jnp.int32), 0)
        slot = source + sz
        for c in range(REC):
            average, is_face = codes == c + 1, codes == c + 33
            hits[c] = hits[c] + jnp.where(average, slot, jnp.where(is_face, slot + 128, 0))
    total = jnp.sum(
        jnp.concatenate(hits, axis=0).astype(jnp.float32), axis=1, keepdims=True
    ).astype(jnp.int32)
    total = jnp.broadcast_to(total, (REC, 128))
    of_face = total > 128
    found[...] = jnp.where(total == 0, NX * NZ, jnp.where(of_face, total - 129, total - 1))
    to_src = local(found, src_s, 10)
    to_src.start()
    load_state.wait()
    load_term.wait()
    for f in range(F):
        base = state_v[f]
        state_v[f] = jnp.where(
            total == 0, base, jnp.where(of_face, base - term_v[f], jnp.zeros_like(base))
        )
    to_src.wait()

    row_total(recv, NX * NZ - 1, rec_s, rec_r).wait()
    for c in range(REC):
        value = recv[jnp.clip(src_s[c, 0], 0, NX * NZ)]
        gathered[pl.ds(c, F, stride=REC), :] = value
    for f in range(F):
        coarse_out[f] = state_v[f] + gathered[pl.ds(REC * f, REC), :]


def store_kernel(fine_v, coarse_v, fine_out, coarse_out, sem):
    copies = [pltpu.make_async_copy(coarse_v, coarse_out, sem.at[2])]
    for h in (0, 1):
        part = fine_out.at[0, :, :, :, pl.ds(128 * h, 128)]
        copies.append(pltpu.make_async_copy(fine_v.at[:, :, h], part, sem.at[h]))
    for c in copies:
        c.start()
    for c in copies:
        c.wait()


def on_device(fine_state, patch_ghosts, coarse_state, coarse_face_term, dest_grp, dest_column):
    any_spec = pl.BlockSpec(memory_space=pl.ANY)
    vmem_spec = pl.BlockSpec(memory_space=pltpu.VMEM)
    vm, sm, f32, i32 = pltpu.VMEM, pltpu.SMEM, jnp.float32, jnp.int32
    dma = pltpu.SemaphoreType.DMA
    fine_new, coarse_new = pl.pallas_call(
        kernel,
        out_shape=(vm((F, 4, 2, 16, 128), f32), vm((F, REC, CZ), f32)),
        in_specs=[any_spec] * 6,
        out_specs=(vmem_spec, vmem_spec),
        scratch_shapes=[
            vm((F, 4, 2, 16, 128), f32),
            vm((2, F, 2, 16, 128), f32),
            vm((F, 8, 4, 8, 128), f32),
            vm((F, 8, 4, 8, 128), f32),
            vm((F, 8, 4, 8, 128), f32),
            vm((F, 8, 4, 8, 128), f32),
            vm((F, 8, 4, 8, 128), f32),
            vm((F, 4, 4, 8, 128), f32),
            vm((F, 4, 8, 128), f32),
            vm((F, 4, 8, 128), f32),
            vm((REC + 1, F, CZ), f32),
            vm((NX * NZ, F, CZ), f32),
            vm((NX * NZ + 1, F, CZ), f32),
            vm((F * REC, CZ), f32),
            vm((1, 128), f32),
            vm((NX, 1, 128), f32),
            vm((1, 128), f32),
            vm((NZ, 1, 128), f32),
            vm((1, 128), i32),
            vm((REC, 128), i32),
            vm((F, REC, CZ), f32),
            vm((F, REC, CZ), f32),
            sm((1, 1, REC), i32),
            sm((1, 1, REC), i32),
            sm((1, 128), i32),
            sm((REC, 128), i32),
            dma((11,)),
            dma((2,)),
            dma((2,)),
            dma,
            dma,
            dma,
            dma,
            dma,
            dma,
            pltpu.SemaphoreType.REGULAR((3,)),
        ],
        compiler_params=pltpu.CompilerParams(collective_id=0, has_side_effects=True),
    )(
        fine_state,
        patch_ghosts,
        coarse_state[0, 0].transpose(1, 0, 2),
        coarse_face_term[0, 0].transpose(1, 0, 2),
        dest_grp,
        dest_column,
    )
    fine_new, coarse_new = pl.pallas_call(
        store_kernel,
        out_shape=(
            jax.ShapeDtypeStruct(fine_state.shape, f32),
            jax.ShapeDtypeStruct((F, REC, CZ), f32),
        ),
        in_specs=[vmem_spec] * 2,
        out_specs=(any_spec, any_spec),
        scratch_shapes=[dma((3,))],
    )(
        pltpu.with_memory_space_constraint(fine_new, vm),
        pltpu.with_memory_space_constraint(coarse_new, vm),
    )
    return fine_new, coarse_new.transpose(1, 0, 2)[None, None]


def solution(mesh):
    in_specs = (
        P("grp", None, "box", None, None),
        P("grp", None, None, None, None, None),
        P("grp", "box", None, None, None),
        P("grp", "box", None, None, None),
        P("grp", "box", None),
        P("grp", "box", None),
    )
    out_specs = (P("grp", None, "box", None, None), P("grp", "box", None, None, None))
    return jax.shard_map(
        on_device, mesh=mesh, in_specs=in_specs, out_specs=out_specs, check_vma=False
    )
```
